512 devices in a mesh: group: 16 (over y_lo, x), sub: 32 (over z, y_hi, core).
Axes of the slice: x: 4, y: 8 (y_hi: 2, y_lo: 4; y = y_hi * 4 + y_lo), z: 8, core: 2. Of those that a mesh axis runs over, the one named last changes fastest.
Arguments:
- initial_condition: bfloat16 [16, 64, 192, 384], P('group', None, 'sub'), may hold values from -6 to 6
- enc_weight: bfloat16 [128, 64], replicated, may hold values from -0.75 to 0.75
- spec_weight: bfloat16 [2, 2, 128, 128], replicated, may hold values from -0.375 to 0.375
- norm_gain: float32 [2, 128], replicated, may hold values from 0.25 to 1.75
- up_weight: bfloat16 [2, 256, 128], replicated, may hold values from -0.5 to 0.5
- down_weight: bfloat16 [2, 128, 256], replicated, may hold values from -0.375 to 0.375
- output_projection_matrix: bfloat16 [64, 128], replicated, may hold values from -0.5 to 0.5
- obs_pos: int32 [32, 16, 512], P('sub', 'group'), may hold values from 0 to 9215
- obs_count: int32 [32, 16], P('sub', 'group'), may hold values from 64 to 512, as said below
- obs_value: float32 [32, 16, 512], P('sub', 'group'), may hold values from -6 to 6
- obs_var: float32 [32, 16, 512], P('sub', 'group'), may hold values from 0.25 to 4
- modulation: float32 [32, 16, 16, 144], P('sub', 'group'), may hold values from -6 to 6
Outputs:
- analysis: bfloat16 [32, 16, 16, 9216], P('sub', 'group')
The draws below stay inside these ranges and needn't reach their ends.
Inputs may be any that keep to these rules, and one draw needn't show every extreme that they name: `obs_count`: at least one tile holds exactly 512 observations.
All inputs are finite; a program needn't handle non-finite values.
Results may differ from the reference program's by a relative error of at most 0.04.
Values may be sent and summed in bfloat16 or wider, within the bound.
A program may use at most 64 MiB of HBM per device.

```python
import math
import jax
import jax.numpy as jnp
from jax import lax

C = 128
HID = 256
PHYSICAL_FIELDS = 64
NLAT = 192
NLON = 384
LMAX = 192
MMAX = 192
MODES = 16
LAYERS = 2
OBS_MAX = 512
REALIZATIONS = 16
PATCH_POINTS = 144
N_GROUP = 16
N_SUB = 32


def draw_obs_count(key, part):
    first_key, second_key, third_key = jax.random.split(key, 3)
    tile_total = N_SUB * N_GROUP
    partial_fill = jax.random.randint(first_key, (tile_total,), OBS_MAX // 8, OBS_MAX // 2 + 1)
    full_tiles = jax.random.randint(second_key, (tile_total,), 0, 8) == 0
    counted = jnp.where(full_tiles, OBS_MAX, partial_fill)
    chosen = jax.random.randint(third_key, (), 0, tile_total)
    counted = counted.at[chosen].set(OBS_MAX)
    return counted.reshape(N_SUB, N_GROUP).astype(jnp.int32)


def place_ends(values, stream_key, least, top_value):
    extent = values.shape
    place = [jax.random.randint(jax.random.fold_in(stream_key, axis), (), 0, extent[axis]) for axis in range(len(extent))]
    values = values.at[tuple(place)].set(least)
    longest = extent.index(max(extent))
    place[longest] = (place[longest] + 1) % extent[longest]
    return values.at[tuple(place)].set(top_value)


def steps_of(key, shape, shards, low, largest):
    def one(axis_at, shards_of):
        draws = jax.random.uniform(jax.random.fold_in(jax.random.fold_in(key, 6), axis_at), (shards_of,), jnp.float32, low / len(shards), largest / len(shards))
        return jnp.repeat(jnp.exp(draws), shape[axis_at] // shards_of).reshape((-1,) + (1,) * (len(shape) - axis_at - 1))

    loudness = one(*shards[0])
    for cut in shards[1:]:
        loudness = loudness * one(*cut)
    return loudness


def centred(stream_key, dims, scale, bound, pieces=(), kind=jnp.bfloat16):
    entries = scale * jax.random.normal(stream_key, dims, jnp.float32)
    if pieces:
        entries = entries * steps_of(stream_key, dims, pieces, -0.22, 0.18)
    return jnp.clip(entries, -bound, bound).astype(kind)


def setup_inputs(seed: int = 0) -> dict:
    key_list = jax.random.split(jax.random.key(seed), 13)
    initial_condition = centred(key_list[0], (REALIZATIONS, PHYSICAL_FIELDS, NLAT, NLON), 1.0, 6.0, ((0, 16), (2, 32)))
    enc_weight = centred(key_list[1], (C, PHYSICAL_FIELDS), PHYSICAL_FIELDS ** -0.5, 0.75)
    spec_weight = centred(key_list[2], (LAYERS, 2, C, C), (2 * C) ** -0.5, 0.375)
    norm_gain = jnp.clip(1.0 + 0.15 * jax.random.normal(key_list[3], (LAYERS, C), jnp.float32), 0.25, 1.75)
    up_weight = centred(key_list[4], (LAYERS, HID, C), C ** -0.5, 0.5)
    down_weight = centred(key_list[5], (LAYERS, C, HID), HID ** -0.5, 0.375)
    output_projection_matrix = centred(key_list[6], (PHYSICAL_FIELDS, C), C ** -0.5, 0.5)
    obs_pos = place_ends(jax.random.randint(key_list[7], (N_SUB, N_GROUP, OBS_MAX), 0, PHYSICAL_FIELDS * PATCH_POINTS), jax.random.fold_in(key_list[7], 1), 0, (PHYSICAL_FIELDS * PATCH_POINTS) - 1).astype(jnp.int32)
    obs_count = draw_obs_count(jax.random.fold_in(key_list[12], 71), 0)
    obs_value = centred(key_list[9], (N_SUB, N_GROUP, OBS_MAX), 1.0, 6.0, ((0, 32), (1, 16)), jnp.float32)
    obs_var = jnp.clip(jnp.exp(math.log(4.0) - 2.7725887 * jax.random.uniform(key_list[10], (N_SUB, N_GROUP, OBS_MAX), jnp.float32) ** steps_of(key_list[10], (N_SUB, N_GROUP, OBS_MAX), ((0, 32), (1, 16)), -0.2, 0.2)), 0.25, 4.0)
    modulation = centred(key_list[11], (N_SUB, N_GROUP, MODES, PATCH_POINTS), 1.0, 6.0, ((0, 32), (1, 16)), jnp.float32)
    return dict(initial_condition=initial_condition, enc_weight=enc_weight, spec_weight=spec_weight, norm_gain=norm_gain, up_weight=up_weight, down_weight=down_weight, output_projection_matrix=output_projection_matrix, obs_pos=obs_pos, obs_count=obs_count, obs_value=obs_value, obs_var=obs_var, modulation=modulation)


def product(pattern, first_operand, second_operand):
    return jnp.einsum(pattern, first_operand.astype(jnp.float32), second_operand.astype(jnp.float32))

def fourier_tables(lon_count, mode_count):
    lon_points = jnp.arange(lon_count, dtype=jnp.int32)
    mode_values = jnp.arange(mode_count, dtype=jnp.int32)
    phase_index = mode_values[:, None] * lon_points[None, :] % lon_count
    angles = phase_index.astype(jnp.float32) * (2.0 * math.pi / lon_count)
    cosine_values = jnp.cos(angles)
    sine_values = jnp.sin(angles)
    forward = jnp.concatenate([cosine_values, -sine_values], axis=0).T / lon_count
    twofold = jnp.where(mode_values == 0, 1.0, 2.0).astype(jnp.float32)[:, None]
    inverse = jnp.stack([twofold * cosine_values, -twofold * sine_values], axis=0)
    return (forward.astype(jnp.bfloat16), inverse.astype(jnp.bfloat16))

def sphere_tables(mode_ids, degree_count, lat_count):
    colatitude = (jnp.arange(lat_count, dtype=jnp.float32) + 0.5) * (math.pi / lat_count)
    cosine_values = jnp.cos(colatitude)[None, :]
    sine_values = jnp.sin(colatitude)[None, :]
    order_value = mode_ids.astype(jnp.float32)[:, None]
    log_start = 0.5 * (jnp.log((2.0 * order_value + 1.0) / (4.0 * math.pi)) + jax.scipy.special.gammaln(order_value + 0.5) - jax.scipy.special.gammaln(order_value + 1.0) - 0.5 * math.log(math.pi)) + order_value * jnp.log(sine_values)
    diagonal_start = jnp.exp(log_start)

    def advance(carried, degree):
        previous, earlier = carried
        degree_value = degree.astype(jnp.float32)
        upper_factor = jnp.sqrt((4.0 * degree_value * degree_value - 1.0) / jnp.maximum(degree_value * degree_value - order_value * order_value, 1.0))
        lower_factor = jnp.sqrt(jnp.maximum((degree_value - 1.0) * (degree_value - 1.0) - order_value * order_value, 0.0) / jnp.maximum(4.0 * (degree_value - 1.0) * (degree_value - 1.0) - 1.0, 1.0))
        recursion = upper_factor * (cosine_values * previous - lower_factor * earlier)
        next_value = jnp.where(degree_value < order_value, 0.0, jnp.where(degree_value == order_value, diagonal_start, jnp.where(degree_value == order_value + 1.0, cosine_values * jnp.sqrt(2.0 * order_value + 3.0) * diagonal_start, recursion)))
        return ((next_value, previous), next_value)
    zero_rows = jnp.zeros((mode_ids.shape[0], lat_count), jnp.float32)
    _, legendre_rows = lax.scan(advance, (zero_rows, zero_rows), jnp.arange(degree_count, dtype=jnp.int32))
    legendre_rows = jnp.transpose(legendre_rows, (1, 0, 2))
    quadrature = 2.0 * math.pi * (math.pi / lat_count) * jnp.sin(colatitude)
    forward = (legendre_rows * quadrature[None, None, :]).astype(jnp.bfloat16)
    inverse = jnp.transpose(legendre_rows, (0, 2, 1)).astype(jnp.bfloat16)
    return (forward, inverse)

def encode(member_state, enc_weight):
    return product('cv,bvyn->bcyn', enc_weight, member_state).astype(jnp.bfloat16)

def to_modes(latent_features, forward_dft):
    zonal = product('bcyn,nk->bcyk', latent_features, forward_dft).astype(jnp.bfloat16)
    return zonal.reshape(latent_features.shape[0], latent_features.shape[1], latent_features.shape[2], 2, forward_dft.shape[1] // 2)

def spectral(columns, legendre_fwd, legendre_inv, mixing):
    coefficients = product('bcyrm,mly->bclrm', columns, legendre_fwd).astype(jnp.bfloat16)
    real_part = product('oc,bclrm->bolrm', mixing[0], coefficients)
    imag_part = product('oc,bclrm->bolrm', mixing[1], coefficients)
    mixed_modes = jnp.stack([real_part[:, :, :, 0] - imag_part[:, :, :, 1], real_part[:, :, :, 1] + imag_part[:, :, :, 0]], axis=3).astype(jnp.bfloat16)
    return product('bclrm,myl->bcyrm', mixed_modes, legendre_inv).astype(jnp.bfloat16)

def finish(latent_features, back, inverse_dft, gain, w_up, w_down):
    summed = latent_features.astype(jnp.float32) + product('bcyrm,rmn->bcyn', back, inverse_dft)
    centered = summed - lax.optimization_barrier(jnp.mean(summed, axis=1, keepdims=True))
    spread = lax.optimization_barrier(jnp.mean(centered * centered, axis=1, keepdims=True))
    normed = (centered * lax.rsqrt(spread + 1e-05) * gain[None, :, None, None]).astype(jnp.bfloat16)
    lifted = jax.nn.gelu(product('hc,bcyn->bhyn', w_up, normed), approximate=False).astype(jnp.bfloat16)
    return (summed + product('ch,bhyn->bcyn', w_down, lifted)).astype(jnp.bfloat16)

def project_features_out(member_state, latent_features, output_projection_matrix):
    return (member_state.astype(jnp.float32) + product('vc,bcyn->bvyn', output_projection_matrix, latent_features)).astype(jnp.bfloat16)

def prepare(patch_realization_fields, positions, values, obs_total, modulation):
    background = patch_realization_fields.astype(jnp.float32)
    member_count = background.shape[0]
    ensemble_mean = lax.optimization_barrier(jnp.sum(background, axis=0)) / member_count
    perturb = background - ensemble_mean[None, :]
    tile_grid_cells = modulation.shape[1]
    is_valid = (jnp.arange(positions.shape[0], dtype=jnp.int32) < obs_total).astype(jnp.float32)
    picked = jnp.take(perturb, positions, axis=1).T
    observed = jnp.take(background, positions, axis=1).T
    mode_at_obs = jnp.take(modulation, positions % tile_grid_cells, axis=1).T
    anomaly_scale = 1.0 / math.sqrt(member_count - 1)
    anomalies = ((is_valid * anomaly_scale)[:, None, None] * picked[:, :, None] * mode_at_obs[:, None, :]).reshape(positions.shape[0], -1)
    innovation = is_valid[:, None] * (values[:, None] - observed)
    return (background, perturb, anomalies, innovation, anomaly_scale)

def cholesky_solve(system, right_side):
    factor = jnp.linalg.cholesky(system)
    partial_solve = jax.scipy.linalg.solve_triangular(factor, right_side, lower=True)
    return jax.scipy.linalg.solve_triangular(factor, partial_solve, lower=True, trans=1)

def weights_ensemble(anomalies, innovation, variances):
    weighted = anomalies / variances[:, None]
    system = jnp.eye(anomalies.shape[1], dtype=jnp.float32) + jnp.dot(anomalies.T, weighted, precision=lax.Precision.HIGHEST)
    return cholesky_solve(system, jnp.dot(weighted.T, innovation, precision=lax.Precision.HIGHEST))

def apply_update(background, perturb, coupling, modulation, anomaly_scale):
    member_count = background.shape[0]
    mode_count = modulation.shape[0]
    variable_count = perturb.shape[1] // modulation.shape[1]
    coupling_table = coupling.reshape(member_count, mode_count, member_count)

    def add_mode(mode_index, summed_terms):
        mode_block = lax.dynamic_index_in_dim(coupling_table, mode_index, axis=1, keepdims=False)
        mode_row = jnp.tile(lax.dynamic_index_in_dim(modulation, mode_index, axis=0, keepdims=False), variable_count)
        return summed_terms + mode_row[None, :] * jnp.dot(mode_block.T, perturb, precision=lax.Precision.HIGHEST)
    summed_terms = lax.fori_loop(0, mode_count, add_mode, jnp.zeros_like(perturb))
    return (background + anomaly_scale * summed_terms).astype(jnp.bfloat16)

def reference(initial_condition, enc_weight, spec_weight, norm_gain, up_weight, down_weight, output_projection_matrix, obs_pos, obs_count, obs_value, obs_var, modulation):
    forward_dft, inverse_dft = fourier_tables(NLON, MMAX)
    legendre_fwd, legendre_inv = sphere_tables(jnp.arange(MMAX, dtype=jnp.int32), LMAX, NLAT)

    def lone_realization(member_state):
        member_state = member_state[None]
        latent_features = encode(member_state, enc_weight)
        for layer_index in range(LAYERS):
            columns = to_modes(latent_features, forward_dft)
            back = spectral(columns, legendre_fwd, legendre_inv, spec_weight[layer_index])
            latent_features = finish(latent_features, back, inverse_dft, norm_gain[layer_index], up_weight[layer_index], down_weight[layer_index])
        return project_features_out(member_state, latent_features, output_projection_matrix)[0]
    predicted_realizations = lax.map(lone_realization, initial_condition)
    patch_realization_fields = predicted_realizations.reshape(REALIZATIONS, PHYSICAL_FIELDS, N_SUB, N_GROUP, PATCH_POINTS)
    patch_realization_fields = jnp.transpose(patch_realization_fields, (2, 3, 0, 1, 4)).reshape(N_SUB * N_GROUP, REALIZATIONS, PHYSICAL_FIELDS * PATCH_POINTS)

    def one_tile(operands):
        members_here, positions, obs_total, values, variances, mode_values = operands
        background, perturb, anomalies, innovation, anomaly_scale = prepare(members_here, positions, values, obs_total, mode_values)
        coupling = weights_ensemble(anomalies, innovation, variances)
        return apply_update(background, perturb, coupling, mode_values, anomaly_scale)
    result = lax.map(one_tile, (patch_realization_fields, obs_pos.reshape(-1, OBS_MAX), obs_count.reshape(-1), obs_value.reshape(-1, OBS_MAX), obs_var.reshape(-1, OBS_MAX), modulation.reshape(-1, MODES, PATCH_POINTS)))
    return result.reshape(N_SUB, N_GROUP, REALIZATIONS, PHYSICAL_FIELDS * PATCH_POINTS)
```

```python
import functools
import math

import jax
import jax.numpy as jnp
import numpy as np
from jax import lax
from jax.experimental import pallas as pl
from jax.experimental.pallas import tpu as pltpu
from jax.sharding import PartitionSpec as P

F32 = jnp.float32
BF16 = jnp.bfloat16
EXACT = lax.Precision.HIGHEST
MESH = pl.DeviceIdType.MESH
NN = ((1,), (0,))
NT = ((1,), (1,))

LATS = 192
LONS = 384
DEGREES = 192
SUB = 32
GROUP = 16
BAND = 6
ROWS = 40
ALL = SUB * ROWS


def dot(a, b, dims, precision=None):
    return lax.dot_general(a, b, (dims, ((), ())), precision=precision, preferred_element_type=F32)


def dft_table():
    m = (BAND * np.arange(SUB)[None, :] + np.arange(BAND)[:, None]).reshape(-1)
    angle = 2.0 * np.pi * ((m[:, None] * np.arange(LONS)[None, :]) % LONS) / LONS
    return np.concatenate([np.cos(angle), -np.sin(angle)], axis=0)


def filter_tables():
    colatitude = (np.arange(LATS) + 0.5) * np.pi / LATS
    x, sine = np.cos(colatitude), np.sin(colatitude)
    m = np.arange(LATS, dtype=np.float64)[:, None]
    gammas = np.array([math.lgamma(v + 0.5) - math.lgamma(v + 1.0) for v in range(LATS)])[:, None]
    start = np.exp(
        0.5 * (np.log((2 * m + 1) / (4 * np.pi)) + gammas - 0.5 * np.log(np.pi)) + m * np.log(sine)[None, :]
    )
    earlier, previous, squares = np.zeros_like(start), np.zeros_like(start), np.zeros_like(start)
    for l in range(DEGREES + 1):
        up = np.sqrt((4.0 * l * l - 1.0) / np.maximum(l * l - m * m, 1.0)) if l else 0.0 * m
        low = np.sqrt(np.maximum((l - 1.0) ** 2 - m * m, 0.0) / max(4.0 * (l - 1.0) ** 2 - 1.0, 1.0))
        value = up * (x[None, :] * previous - low * earlier)
        value = np.where(l == m + 1, x[None, :] * np.sqrt(2 * m + 3) * start, value)
        value = np.where(l == m, start, np.where(l < m, 0.0, value))
        earlier, previous = previous, value
        if l < DEGREES:
            squares += value * value
    weight = 2.0 * np.pi * (np.pi / LATS) * sine[None, :] * np.where(m == 0, 1.0, 2.0) / LONS
    e = np.sqrt((DEGREES**2 - m * m) / (4.0 * DEGREES**2 - 1.0))
    per_order = [previous * e * weight, earlier * e * weight, squares * weight, previous, earlier]
    order = np.zeros((SUB, 8, SUB, ROWS), np.float32)
    place = np.zeros((8, SUB, ROWS), np.float32)
    place[2], place[3] = -1.0, -2.0
    for mm in range(BAND):
        for i in range(BAND):
            at = mm * BAND + i
            lats = BAND * np.arange(SUB) + i
            for k, table in enumerate(per_order):
                order[:, k, :, at] = table[BAND * np.arange(SUB) + mm][:, lats]
            high = x[lats].astype(np.float32)
            place[0, :, at], place[1, :, at] = high, x[lats] - high.astype(np.float64)
            place[2, :, at] = place[3, :, at] = mm
            place[4, :, at] = lats
    return order.reshape(SUB, 8, ALL), place.reshape(8, ALL)


def erf_gelu(x):
    return 0.5 * x * (1.0 + lax.erf(x * (1.0 / math.sqrt(2.0))))


def forecast_kernel(
    ic_ref, enc_ref, spec_ref, gain_ref, up_ref, down_ref, proj_ref, dft_ref, place_ref, order_hbm, out_ref,
    raw, member, filt, order, cols, gain, mix, spread, sent0, got0, sent1, got1, sent2, got2, sent3, got3,
    hidden, cast, tiles, send_sem, recv_sem, gsend_sem, grecv_sem, local_sem,
):
    me = lax.axis_index("sub")
    mine = lax.axis_index("group")

    def sub_peer(d):
        return lax.rem(me + d, SUB)

    def group_peer(d):
        return lax.rem(mine + d, GROUP)

    barrier = pltpu.get_barrier_semaphore()

    def greet_sub(d, _):
        pl.semaphore_signal(barrier, inc=1, device_id={"sub": sub_peer(d)}, device_id_type=MESH)
        return 0

    def greet_group(d, _):
        pl.semaphore_signal(barrier, inc=1, device_id={"group": group_peer(d)}, device_id_type=MESH)
        return 0

    lax.fori_loop(1, SUB, greet_sub, 0)
    lax.fori_loop(1, GROUP, greet_group, 0)
    fetch = pltpu.make_async_copy(order_hbm.at[me], order, local_sem.at[0])
    fetch.start()

    def exchange(stage, sent, got):
        def copy(d):
            return pltpu.make_async_remote_copy(
                src_ref=sent.at[sub_peer(d)], dst_ref=got.at[me], send_sem=send_sem.at[stage, d],
                recv_sem=recv_sem.at[stage, d], device_id={"sub": sub_peer(d)}, device_id_type=MESH)

        def start(d, _):
            copy(d).start()
            return 0

        def finish(d, _):
            copy(d).wait()
            return 0

        return (lambda: lax.fori_loop(1, SUB, start, 0)), (lambda: lax.fori_loop(1, SUB, finish, 0))

    def unpack(v, _):
        fields = ic_ref[v].astype(F32)
        for l in range(3):
            raw[l, pl.ds(pl.multiple_of(v * 8, 8), BAND), :] = fields[:, l * 128:(l + 1) * 128]
        return 0

    lax.fori_loop(0, 64, unpack, 0, unroll=4)
    spread[...] = jnp.zeros_like(spread)
    empty = jnp.zeros((64, LONS), BF16)

    def first_dft(i, _):
        fields = jnp.concatenate([raw[l, pl.ds(i, 64, stride=8), :] for l in range(3)], axis=1).astype(BF16)
        member[i] = fields
        real = jnp.concatenate([fields, empty], axis=0)
        imag = jnp.concatenate([empty, fields], axis=0)
        zonal = dot(dft_ref[0:192, :], real, NT) + dot(dft_ref[192:384, :], imag, NT)
        for mm in range(BAND):
            spread[0, pl.ds(mm * BAND + i, SUB, stride=ROWS), :] = zonal[mm * SUB:(mm + 1) * SUB, :]
        return 0

    lax.fori_loop(0, BAND, first_dft, 0)

    def stage_out(d, _):
        sent0[d] = spread[0, pl.ds(pl.multiple_of(d * ROWS, 8), ROWS), :].astype(BF16)
        return 0

    lax.fori_loop(0, SUB, stage_out, 0, unroll=4)
    pl.semaphore_wait(barrier, SUB + GROUP - 2)
    start, finish = exchange(0, sent0, got0)
    start()
    got0[me] = sent0[me]

    fetch.wait()
    cols[...] = jnp.concatenate([order[...], place_ref[...], jnp.zeros((112, ALL), F32)], axis=0).T

    def build(b, _):
        at = pl.ds(pl.multiple_of(b * 16, 16), 16)
        col = cols[at, :]
        top = col[:, 3:4] * order[1:2, :] - col[:, 4:5] * order[0:1, :]
        gap = (col[:, 8:9] - place_ref[0:1, :]) + (col[:, 9:10] - place_ref[1:2, :])
        same = col[:, 12:13] == place_ref[4:5, :]
        value = jnp.where(same, order[2:3, :], top / jnp.where(same, 1.0, gap))
        filt[at, :] = jnp.where(col[:, 11:12] == place_ref[2:3, :], value, 0.0).astype(BF16)
        return 0

    lax.fori_loop(0, ALL // 16, build, 0)
    gain[...] = jnp.concatenate([gain_ref[...], jnp.zeros((126, 128), F32)], axis=0).T
    enc = enc_ref[...]
    none = jnp.zeros((128, 64), BF16)
    enc_real = jnp.concatenate([enc, none], axis=1)
    enc_imag = jnp.concatenate([none, enc], axis=1)
    mix[0] = (dot(spec_ref[0, 0], enc_real, NN) - dot(spec_ref[0, 1], enc_imag, NN)).astype(BF16)
    mix[1] = (dot(spec_ref[0, 1], enc_real, NN) + dot(spec_ref[0, 0], enc_imag, NN)).astype(BF16)

    finish()

    def stage_in(got, part, dest):
        def body(d, _):
            block = got[d] if part is None else got[d, part]
            dest[pl.ds(pl.multiple_of(d * ROWS, 8), ROWS), :] = block.astype(F32)
            return 0
        lax.fori_loop(0, SUB, body, 0, unroll=4)

    stage_in(got0, None, spread.at[0])
    source = spread[0].astype(BF16)
    for b in range(4):
        filtered = dot(filt[b * 320:(b + 1) * 320, :], source, NN)
        for k in range(8):
            sent1[b * 8 + k] = filtered[k * ROWS:(k + 1) * ROWS, :].astype(BF16)
    start, finish = exchange(1, sent1, got1)
    start()
    got1[me] = sent1[me]
    finish()

    def latitude(i, part):
        return jnp.concatenate(
            [spread[part, pl.ds(mm * BAND + i, SUB, stride=ROWS), :] for mm in range(BAND)], axis=0).astype(BF16)

    def pointwise(layer, summed):
        centred = summed - jnp.mean(summed, axis=0, keepdims=True)
        spread_of = jnp.mean(centred * centred, axis=0, keepdims=True)
        normed = (centred * lax.rsqrt(spread_of + 1e-05) * gain[:, layer:layer + 1]).astype(BF16)
        lifted = erf_gelu(dot(up_ref[layer], normed, NN)).astype(BF16)
        return (summed + dot(down_ref[layer], lifted, NN)).astype(BF16)

    stage_in(got1, None, spread.at[0])

    def first_back(i, _):
        back = latitude(i, 0)
        real = dot(mix[0], back, NT).astype(BF16)
        imag = dot(mix[1], back, NT).astype(BF16)
        summed = dot(enc_ref[...], member[i], NN)
        summed = summed + dot(real, dft_ref[0:192, :], NN) + dot(imag, dft_ref[192:384, :], NN)
        hidden[i] = pointwise(0, summed)
        return 0

    lax.fori_loop(0, BAND, first_back, 0)

    def second_dft(i, _):
        zonal = dot(dft_ref[...], hidden[i], NT)
        for part in range(2):
            for mm in range(BAND):
                at = part * 192 + mm * SUB
                spread[part, pl.ds(mm * BAND + i, SUB, stride=ROWS), :] = zonal[at:at + SUB, :]
        return 0

    spread[...] = jnp.zeros_like(spread)
    lax.fori_loop(0, BAND, second_dft, 0)

    def stage_out2(d, _):
        for part in range(2):
            sent2[d, part] = spread[part, pl.ds(pl.multiple_of(d * ROWS, 8), ROWS), :].astype(BF16)
        return 0

    lax.fori_loop(0, SUB, stage_out2, 0, unroll=2)
    start, finish = exchange(2, sent2, got2)
    start()
    got2[me] = sent2[me]
    finish()
    stage_in(got2, 0, spread.at[0])
    stage_in(got2, 1, spread.at[1])
    source = jnp.concatenate([spread[0].astype(BF16), spread[1].astype(BF16)], axis=1)
    for b in range(4):
        filtered = dot(filt[b * 320:(b + 1) * 320, :], source, NN)
        for k in range(8):
            for part in range(2):
                sent3[b * 8 + k, part] = filtered[k * ROWS:(k + 1) * ROWS, part * 128:(part + 1) * 128].astype(BF16)
    start, finish = exchange(3, sent3, got3)
    start()
    got3[me] = sent3[me]
    finish()
    stage_in(got3, 0, spread.at[0])
    stage_in(got3, 1, spread.at[1])

    def second_back(i, _):
        back_real = latitude(i, 0)
        back_imag = latitude(i, 1)
        w_real, w_imag = spec_ref[1, 0], spec_ref[1, 1]
        real = (dot(w_real, back_real, NT) - dot(w_imag, back_imag, NT)).astype(BF16)
        imag = (dot(w_imag, back_real, NT) + dot(w_real, back_imag, NT)).astype(BF16)
        summed = hidden[i].astype(F32)
        summed = summed + dot(real, dft_ref[0:192, :], NN) + dot(imag, dft_ref[192:384, :], NN)
        fields = member[i].astype(F32) + dot(proj_ref[...], pointwise(1, summed), NN)
        for l in range(3):
            cast[3 * i + l] = fields[:, l * 128:(l + 1) * 128]
        return 0

    lax.fori_loop(0, BAND, second_back, 0)

    lane = lax.broadcasted_iota(jnp.int32, (8, 128), 1)

    def window(w, begin):
        first, turn = begin // 128, begin % 128
        def piece(j):
            return cast[min(max(j, 0), 17), pl.ds(w, 8, stride=8), :]
        if turn == 0:
            return piece(first)
        return jnp.where(
            lane < 128 - turn, pltpu.roll(piece(first), 128 - turn, 1), pltpu.roll(piece(first + 1), 128 - turn, 1))

    for g in range(GROUP):
        columns = []
        for t in range(9):
            value = window(t, 144 * g - 16 * t) if t < 8 else None
            if t > 0:
                before = window(t - 1, 144 * (g + 1) - 16 * t)
                value = before if value is None else jnp.where(lane < 16 * t, before, value)
            columns.append(value)
        tiles[g] = jnp.concatenate(columns, axis=0).astype(BF16)

    def tile_copy(d):
        return pltpu.make_async_remote_copy(
            src_ref=tiles.at[group_peer(d)], dst_ref=out_ref.at[mine], send_sem=gsend_sem.at[d],
            recv_sem=grecv_sem.at[d], device_id={"group": group_peer(d)}, device_id_type=MESH)

    def tile_start(d, _):
        tile_copy(d).start()
        return 0

    def tile_finish(d, _):
        tile_copy(d).wait()
        return 0

    own = pltpu.make_async_copy(tiles.at[mine], out_ref.at[mine], local_sem.at[1])
    own.start()
    lax.fori_loop(1, GROUP, tile_start, 0)
    own.wait()
    lax.fori_loop(1, GROUP, tile_finish, 0)


def forecast(ic, enc, spec, gain, up, down, proj):
    order, place = filter_tables()
    v = pl.BlockSpec(memory_space=pltpu.VMEM)
    block = (SUB, ROWS, 128)
    pair = (SUB, 2, ROWS, 128)
    return pl.pallas_call(
        forecast_kernel,
        out_shape=jax.ShapeDtypeStruct((GROUP, 72, 128), BF16),
        in_specs=[v] * 9 + [pl.BlockSpec(memory_space=pl.ANY)],
        out_specs=pl.BlockSpec(memory_space=pl.ANY),
        scratch_shapes=[
            pltpu.VMEM((3, 512, 128), F32),
            pltpu.VMEM((BAND, 64, LONS), BF16),
            pltpu.VMEM((ALL, ALL), BF16),
            pltpu.VMEM((8, ALL), F32),
            pltpu.VMEM((ALL, 128), F32),
            pltpu.VMEM((128, 128), F32),
            pltpu.VMEM((2, 128, 128), BF16),
            pltpu.VMEM((2, ALL, 128), F32),
            pltpu.VMEM(block, BF16), pltpu.VMEM(block, BF16), pltpu.VMEM(block, BF16), pltpu.VMEM(block, BF16),
            pltpu.VMEM(pair, BF16), pltpu.VMEM(pair, BF16), pltpu.VMEM(pair, BF16), pltpu.VMEM(pair, BF16),
            pltpu.VMEM((BAND, 128, LONS), BF16),
            pltpu.VMEM((18, 64, 128), F32),
            pltpu.VMEM((GROUP, 72, 128), BF16),
            pltpu.SemaphoreType.DMA((4, SUB)), pltpu.SemaphoreType.DMA((4, SUB)),
            pltpu.SemaphoreType.DMA((GROUP,)), pltpu.SemaphoreType.DMA((GROUP,)),
            pltpu.SemaphoreType.DMA((2,)),
        ],
        compiler_params=pltpu.CompilerParams(collective_id=0, has_side_effects=True, vmem_limit_bytes=48 << 20),
        name="forecast",
    )(ic, enc, spec, gain, up, down, proj, jnp.asarray(dft_table(), BF16), jnp.asarray(place), jnp.asarray(order))


def reduce_rows(pieces):
    rows = [[p[a:a + 1, :] for p in pieces] for a in range(8)]
    d = [[jnp.broadcast_to(rows[a][0][:, b:b + 1], (1, 128)) for b in range(8)] for a in range(8)]
    for a in range(8):
        inv = 1.0 / d[a][a]
        rows[a] = [x * inv for x in rows[a]]
        top = [None if b <= a else d[a][b] * inv for b in range(8)]
        d[a] = top
        for c in range(8):
            if c == a:
                continue
            f = d[c][a]
            rows[c] = [x - f * y for x, y in zip(rows[c], rows[a])]
            d[c] = [d[c][b] if b <= a else d[c][b] - f * top[b] for b in range(8)]
    return [jnp.concatenate([rows[a][l] for a in range(8)], axis=0) for l in range(len(pieces))]


def jordan(sys_ref, n, width):
    pieces = width // 128
    blocks = n // 8
    heads = n // 128
    def shift(vals, rows):
        lane = lax.broadcasted_iota(jnp.int32, (rows, 128), 1)
        r = [pltpu.roll(v, 120, 1) for v in vals[:heads]]
        if heads == 1:
            return r + list(vals[1:])
        return [jnp.where(lane < 120, r[h], r[(h + 1) % heads]) for h in range(heads)] + list(vals[heads:])
    def load(r):
        at = pl.ds(pl.multiple_of(r * 8, 8), 8)
        return [sys_ref[at, l * 128:(l + 1) * 128] for l in range(pieces)]
    def step(blk, red):
        nxt = lax.rem(blk + 1, blocks)
        x = load(nxt)
        c = [jnp.broadcast_to(x[0][:, b:b + 1], (8, 128)) for b in range(8)]
        for b in range(8):
            x = [v - c[b] * r[b:b + 1, :] for v, r in zip(x, red)]
        new = reduce_rows(shift(x, 8))
        left = sys_ref[:, 0:8]
        full = [sys_ref[:, l * 128:(l + 1) * 128] - dot(left, red[l], NN, EXACT) for l in range(pieces)]
        full = shift(full, n)
        for l in range(pieces):
            sys_ref[:, l * 128:(l + 1) * 128] = full[l]
        keep = shift(list(red), 8)
        at = pl.ds(pl.multiple_of(blk * 8, 8), 8)
        for l in range(pieces):
            sys_ref[at, l * 128:(l + 1) * 128] = keep[l]
        return tuple(new)
    lax.fori_loop(0, blocks, step, tuple(reduce_rows(load(0))))


def analysis_kernel(tile_ref, count_ref, pos_ref, val_ref, var_ref, mod_ref, out_ref, raw, state, pert, sysm, mtab):
    for q in range(16):
        raw[q * 72:(q + 1) * 72, :] = tile_ref[q].astype(F32)
    def collect(r, _):
        rows = raw[pl.ds(r, 16, stride=72), :]
        at = pl.ds(pl.multiple_of(r * 16, 16), 16)
        state[at, :] = rows
        mean = jnp.sum(rows, axis=0, keepdims=True) * (1.0 / 16)
        pert[at, :] = rows - mean
        return 0
    lax.fori_loop(0, 72, collect, 0, unroll=8)
    pos = pos_ref[...]
    col = pos >> 7
    lane = pos & 127
    u = jnp.floor((col.astype(F32) + 0.5) * (1.0 / 9)).astype(jnp.int32)
    row = (col - 9 * u) * 8 + u
    cell = pos - 144 * jnp.floor((pos.astype(F32) + 0.5) * (1.0 / 144)).astype(jnp.int32)
    pick = (lax.broadcasted_iota(jnp.int32, (128, 512), 0) == lane).astype(F32).astype(BF16)
    pick_cell = (lax.broadcasted_iota(jnp.int32, (144, 512), 0) == cell).astype(F32).astype(BF16)
    def gather(i, acc):
        at = pl.ds(pl.multiple_of(i * 128, 128), 128)
        part = dot(state[at, :].astype(BF16), pick, NN)
        for k in range(8):
            acc = acc + jnp.where(row == i * 8 + k, part[k * 16:(k + 1) * 16, :], 0.0)
        return acc
    picked = lax.fori_loop(0, 9, gather, jnp.zeros((16, 512), F32))
    mod = mod_ref[...]
    hi = mod.astype(BF16)
    rest = mod - hi.astype(F32)
    mid = rest.astype(BF16)
    low = (rest - mid.astype(F32)).astype(BF16)
    mod_at = dot(hi, pick_cell, NN) + dot(mid, pick_cell, NN) + dot(low, pick_cell, NN)
    valid = lax.broadcasted_iota(jnp.int32, (1, 512), 1) < count_ref[0, 0]
    root = jnp.where(valid, lax.rsqrt(var_ref[...]), 0.0)
    dev = (picked - jnp.sum(picked, axis=0, keepdims=True) * (1.0 / 16)) * (root * (1.0 / math.sqrt(15.0)))
    innov = jnp.where(valid, val_ref[...] - picked, 0.0) * root
    anom = jnp.concatenate([dev[k:k + 1, :] * mod_at for k in range(16)], axis=0)
    eye = (lax.broadcasted_iota(jnp.int32, (256, 256), 0) == lax.broadcasted_iota(jnp.int32, (256, 256), 1)).astype(F32)
    sysm[:, 0:256] = dot(anom, anom, NT, EXACT) + eye
    rhs = jnp.concatenate([innov, jnp.zeros((112, 512), F32)], axis=0)
    sysm[:, 256:384] = dot(anom, rhs, NT, EXACT)
    jordan(sysm, 256, 384)
    wt = sysm[:, 256:384].T[0:16, :]
    spread = jnp.concatenate([wt] * 16, axis=0)
    same = (lax.broadcasted_iota(jnp.int32, (256, 256), 0) // 16) == (lax.broadcasted_iota(jnp.int32, (256, 256), 1) // 16)
    spread = jnp.where(same, spread, 0.0)
    modk = jnp.concatenate([mod * (1.0 / math.sqrt(15.0))] * 16, axis=0)
    coef = dot(spread, modk, NN, EXACT)
    for t in range(9):
        start = (128 * t) % 144
        if start + 128 <= 144:
            part = coef[:, start:start + 128]
        else:
            part = jnp.concatenate([coef[:, start:144], coef[:, 0:start - 16]], axis=1)
        mtab[t] = part
    def apply(t, _):
        for u8 in range(8):
            at = pl.multiple_of((t * 8 + u8) * 16, 16)
            acc = state[pl.ds(at, 16), :]
            p = pert[pl.ds(at, 16), :]
            for k in range(16):
                acc = acc + mtab[t, k * 16:(k + 1) * 16, :] * p[k:k + 1, :]
            out_ref[:, pl.ds(pl.multiple_of((9 * u8 + t) * 128, 128), 128)] = acc.astype(BF16)
        return 0
    lax.fori_loop(0, 9, apply, 0)


def analysis(tile, count, pos, val, var, mod):
    v = pl.BlockSpec(memory_space=pltpu.VMEM)
    return pl.pallas_call(
        analysis_kernel,
        out_shape=jax.ShapeDtypeStruct((16, 9216), BF16),
        in_specs=[v, pl.BlockSpec(memory_space=pltpu.SMEM), v, v, v, v],
        out_specs=v,
        scratch_shapes=[pltpu.VMEM((1152, 128), F32), pltpu.VMEM((1152, 128), F32), pltpu.VMEM((1152, 128), F32),
                        pltpu.VMEM((256, 384), F32), pltpu.VMEM((9, 256, 128), F32)],
        compiler_params=pltpu.CompilerParams(vmem_limit_bytes=48 << 20),
        name="analysis",
    )(tile, count, pos, val, var, mod)


def shards(ic, enc, spec, gain, up, down, proj, pos, count, value, var, mod):
    tile = forecast(ic[0], enc, spec, gain, up, down, proj)
    out = analysis(tile, count, pos[0], value[0], var[0], mod[0, 0])
    return out[None, None]


def solution(mesh):
    part = P("sub", "group", None)
    return jax.shard_map(
        shards,
        mesh=mesh,
        in_specs=(P("group", None, "sub", None),) + (P(),) * 6
        + (part, P("sub", "group"), part, part, P("sub", "group", None, None)),
        out_specs=P("sub", "group", None, None),
        check_vma=False,
    )
```

```python
import functools
import math

import jax
import jax.numpy as jnp
import numpy as np
from jax import lax
from jax.experimental import pallas as pl
from jax.experimental.pallas import tpu as pltpu
from jax.sharding import PartitionSpec as P

F32 = jnp.float32
BF16 = jnp.bfloat16
EXACT = lax.Precision.HIGHEST
MESH = pl.DeviceIdType.MESH
NN = ((1,), (0,))
NT = ((1,), (1,))

LATS = 192
LONS = 384
DEGREES = 192
SUB = 32
GROUP = 16
BAND = 6
HALF = BAND // 2
USED = HALF * BAND
GAP = 24
ROWS = 2 * GAP
ALL = SUB * ROWS


def dot(a, b, dims, precision=None):
    return lax.dot_general(a, b, (dims, ((), ())), precision=precision, preferred_element_type=F32)


def dft_table():
    m = (BAND * np.arange(SUB)[None, :] + np.arange(BAND)[:, None]).reshape(-1)
    angle = 2.0 * np.pi * ((m[:, None] * np.arange(LONS)[None, :]) % LONS) / LONS
    return np.concatenate([np.cos(angle), -np.sin(angle)], axis=0)


def filter_tables():
    colatitude = (np.arange(LATS) + 0.5) * np.pi / LATS
    x, sine = np.cos(colatitude), np.sin(colatitude)
    m = np.arange(LATS, dtype=np.float64)[:, None]
    gammas = np.array([math.lgamma(v + 0.5) - math.lgamma(v + 1.0) for v in range(LATS)])[:, None]
    start = np.exp(
        0.5 * (np.log((2 * m + 1) / (4 * np.pi)) + gammas - 0.5 * np.log(np.pi)) + m * np.log(sine)[None, :]
    )
    earlier, previous, squares = np.zeros_like(start), np.zeros_like(start), np.zeros_like(start)
    for l in range(DEGREES + 1):
        up = np.sqrt((4.0 * l * l - 1.0) / np.maximum(l * l - m * m, 1.0)) if l else 0.0 * m
        low = np.sqrt(np.maximum((l - 1.0) ** 2 - m * m, 0.0) / max(4.0 * (l - 1.0) ** 2 - 1.0, 1.0))
        value = up * (x[None, :] * previous - low * earlier)
        value = np.where(l == m + 1, x[None, :] * np.sqrt(2 * m + 3) * start, value)
        value = np.where(l == m, start, np.where(l < m, 0.0, value))
        earlier, previous = previous, value
        if l < DEGREES:
            squares += value * value
    weight = 2.0 * np.pi * (np.pi / LATS) * sine[None, :] * np.where(m == 0, 1.0, 2.0) / LONS
    e = np.sqrt((DEGREES**2 - m * m) / (4.0 * DEGREES**2 - 1.0))
    per_order = [previous * e * weight, earlier * e * weight, squares * weight, previous, earlier]
    order = np.zeros((SUB, BAND, 8, 256), np.float32)
    place = np.zeros((8, 256), np.float32)
    place[0] = 2.0 + np.arange(256)
    lats = (BAND * np.arange(SUB)[None, :] + np.arange(BAND)[:, None]).reshape(-1)
    for k, table in enumerate(per_order):
        order[:, :, k, :LATS] = table.reshape(SUB, BAND, LATS)[:, :, lats]
    place[0, :LATS] = x[lats].astype(np.float32)
    place[1, :LATS] = x[lats] - x[lats].astype(np.float32).astype(np.float64)
    place[2] = np.arange(256)
    return order, place


def erf_gelu(x):
    return 0.5 * x * (1.0 + lax.erf(x * (1.0 / math.sqrt(2.0))))


def forecast_kernel(
    ic_hbm, enc_hbm, spec_hbm, gain_hbm, up_hbm, down_hbm, proj_hbm, dft_hbm, place_hbm, order_hbm, out_ref,
    fields, enc_ref, spec_ref, gain_ref, up_ref, down_ref, proj_ref, dft_ref, place_ref, order_ref,
    filt, gain, mix, spread, result, source, sent0, got0, sent1, got1, sent2, got2, sent3, got3,
    hidden, cast, tiles, send_sem, recv_sem, tile_send, tile_recv, local_sem,
):
    group = lax.axis_index("group")
    sub = lax.axis_index("sub")

    barrier = pltpu.get_barrier_semaphore()

    def greet_subs(d, _):
        pl.semaphore_signal(barrier, inc=1, device_id=(group, (sub + d) % SUB), device_id_type=MESH)
        return 0

    def greet_tiles(d, _):
        pl.semaphore_signal(barrier, inc=1, device_id=((group + d) % GROUP, sub), device_id_type=MESH)
        return 0

    lax.fori_loop(1, SUB, greet_subs, 0)
    lax.fori_loop(1, GROUP, greet_tiles, 0)

    loads = {}
    for n, (name, src, dst) in enumerate((
        ("fields", ic_hbm, fields), ("dft", dft_hbm, dft_ref), ("order", order_hbm.at[sub], order_ref),
        ("place", place_hbm, place_ref), ("enc", enc_hbm, enc_ref), ("spec", spec_hbm, spec_ref),
        ("gain", gain_hbm, gain_ref), ("up", up_hbm, up_ref), ("down", down_hbm, down_ref),
        ("proj", proj_hbm, proj_ref),
    )):
        loads[name] = pltpu.make_async_copy(src, dst, local_sem.at[n])
        loads[name].start()

    class Exchange:
        def __init__(self, stage, sent, got):
            self.stage, self.sent, self.got = stage, sent, got

        def copy(self, half, d):
            band = (sub + d) % SUB
            return pltpu.make_async_remote_copy(
                src_ref=self.sent.at[band, half], dst_ref=self.got.at[sub, half],
                send_sem=send_sem.at[self.stage * 2 + half, d], recv_sem=recv_sem.at[self.stage * 2 + half, d],
                device_id=(group, band), device_id_type=MESH)

        def start(self, half):
            def body(d, _):
                self.copy(half, d).start()
                return 0

            lax.fori_loop(1, SUB, body, 0)
            self.got[sub, half] = self.sent[sub, half]

        def finish(self, half):
            def body(d, _):
                self.copy(half, d).wait()
                return 0

            lax.fori_loop(1, SUB, body, 0)

    def row_of(i, mm):
        return (i // HALF) * GAP + (i % HALF) * BAND + mm

    def put(dest, i, mm, rows):
        dest[pl.ds(row_of(i, mm), SUB, stride=ROWS), :] = rows

    def take(src, i, mm):
        return src[pl.ds(row_of(i, mm), SUB, stride=ROWS), :]

    def stage_out(src, sent, half, part):
        def body(d, _):
            block = src[pl.ds(pl.multiple_of(d * ROWS + half * GAP, 8), USED), :].astype(BF16)
            if part is None:
                sent[d, half] = block
            else:
                sent[d, half, part] = block
            return 0
        lax.fori_loop(0, SUB, body, 0, unroll=8)

    def stage_in(got, half, part, dest):
        def body(d, _):
            block = got[d, half] if part is None else got[d, half, part]
            dest[pl.ds(pl.multiple_of(d * ROWS + half * GAP, 8), USED), :] = block.astype(F32)
            return 0
        lax.fori_loop(0, SUB, body, 0, unroll=8)

    halves = [range(0, HALF), range(HALF, BAND)]
    first, second = Exchange(0, sent0, got0), Exchange(1, sent1, got1)
    third, fourth = Exchange(2, sent2, got2), Exchange(3, sent3, got3)
    empty = jnp.zeros((64, LONS), BF16)
    loads["fields"].wait()
    loads["dft"].wait()
    for half in range(2):
        for i in halves[half]:
            here = fields[i]
            real = jnp.concatenate([here, empty], axis=0)
            imag = jnp.concatenate([empty, here], axis=0)
            zonal = dot(dft_ref[0:192, :], real, NT) + dot(dft_ref[192:384, :], imag, NT)
            for mm in range(BAND):
                put(spread.at[0], i, mm, zonal[mm * SUB:(mm + 1) * SUB, :])
        stage_out(spread.at[0], sent0, half, None)
        if half == 0:
            pl.semaphore_wait(barrier, SUB + GROUP - 2)
        first.start(half)

    loads["order"].wait()
    loads["place"].wait()
    for mm in range(BAND):
        rows = order_ref[mm]
        col = jnp.concatenate([rows, place_ref[...], jnp.zeros((112, 256), F32)], axis=0).T[0:LATS, :]
        for b in range(4):
            c = col[b * 48:(b + 1) * 48, :]
            top = c[:, 3:4] * rows[1:2, :] - c[:, 4:5] * rows[0:1, :]
            gap = (c[:, 8:9] - place_ref[0:1, :]) + (c[:, 9:10] - place_ref[1:2, :])
            same = c[:, 10:11] == place_ref[2:3, :]
            value = jnp.where(same, rows[2:3, :], top / jnp.where(same, 1.0, gap))
            filt[mm, b * 48:(b + 1) * 48, :] = value.astype(BF16)
    for name in ("enc", "spec", "gain", "up", "down", "proj"):
        loads[name].wait()
    gain[...] = jnp.concatenate([gain_ref[...], jnp.zeros((126, 128), F32)], axis=0).T
    enc = enc_ref[...].T
    none = jnp.zeros((128, 64), BF16)
    enc_real = jnp.concatenate([enc, none], axis=1)
    enc_imag = jnp.concatenate([none, enc], axis=1)
    mix[0] = (dot(spec_ref[0, 0], enc_real, NN) - dot(spec_ref[0, 1], enc_imag, NN)).astype(BF16)
    mix[1] = (dot(spec_ref[0, 1], enc_real, NN) + dot(spec_ref[0, 0], enc_imag, NN)).astype(BF16)

    def latitude(i, part):
        return jnp.concatenate([take(spread.at[part], i, mm) for mm in range(BAND)], axis=0).astype(BF16)

    def apply_filter(parts, sent, exchange):
        for mm in range(BAND):
            for part in range(parts):
                source[mm, :, part * 128:(part + 1) * 128] = jnp.concatenate(
                    [take(spread.at[part], i, mm) for i in range(BAND)], axis=0).astype(BF16)
        for half in range(2):
            for mm in range(BAND):
                filtered = dot(filt[mm, half * 96:(half + 1) * 96, 0:LATS], source[mm, :, 0:parts * 128], NN)
                for part in range(parts):
                    for k, i in enumerate(halves[half]):
                        put(result.at[part], i, mm, filtered[k * SUB:(k + 1) * SUB, part * 128:(part + 1) * 128])
            for part in range(parts):
                stage_out(result.at[part], sent, half, part if parts > 1 else None)
            exchange.start(half)

    for half in range(2):
        first.finish(half)
        stage_in(got0, half, None, spread.at[0])
    apply_filter(1, sent1, second)

    def pointwise(layer, summed):
        centred = summed - jnp.mean(summed, axis=0, keepdims=True)
        spread_of = jnp.mean(centred * centred, axis=0, keepdims=True)
        normed = (centred * lax.rsqrt(spread_of + 1e-05) * gain[:, layer:layer + 1]).astype(BF16)
        lifted = erf_gelu(dot(up_ref[layer], normed, NN)).astype(BF16)
        return (summed + dot(down_ref[layer], lifted, NN)).astype(BF16)

    for half in range(2):
        second.finish(half)
        stage_in(got1, half, None, spread.at[0])
        for i in halves[half]:
            back = latitude(i, 0)
            real = dot(mix[0], back, NT).astype(BF16)
            imag = dot(mix[1], back, NT).astype(BF16)
            summed = dot(enc, fields[i], NN)
            summed = summed + dot(real, dft_ref[0:192, :], NN) + dot(imag, dft_ref[192:384, :], NN)
            after = pointwise(0, summed)
            hidden[i] = after
            zonal = dot(dft_ref[...], after, NT)
            for part in range(2):
                for mm in range(BAND):
                    at = part * 192 + mm * SUB
                    put(result.at[part], i, mm, zonal[at:at + SUB, :])
        for part in range(2):
            stage_out(result.at[part], sent2, half, part)
        third.start(half)

    for half in range(2):
        third.finish(half)
        for part in range(2):
            stage_in(got2, half, part, spread.at[part])
    apply_filter(2, sent3, fourth)

    def second_back(i):
        back_real = latitude(i, 0)
        back_imag = latitude(i, 1)
        w_real, w_imag = spec_ref[1, 0], spec_ref[1, 1]
        real = (dot(w_real, back_real, NT) - dot(w_imag, back_imag, NT)).astype(BF16)
        imag = (dot(w_imag, back_real, NT) + dot(w_real, back_imag, NT)).astype(BF16)
        summed = hidden[i].astype(F32)
        summed = summed + dot(real, dft_ref[0:192, :], NN) + dot(imag, dft_ref[192:384, :], NN)
        ahead = fields[i].astype(F32) + dot(proj_ref[...], pointwise(1, summed), NN)
        for l in range(3):
            cast[3 * i + l] = ahead[:, l * 128:(l + 1) * 128]

    lane = lax.broadcasted_iota(jnp.int32, (8, 128), 1)

    def window(w, begin):
        first, turn = begin // 128, begin % 128
        def piece(j):
            return cast[min(max(j, 0), 17), pl.ds(w, 8, stride=8), :]
        if turn == 0:
            return piece(first)
        return jnp.where(
            lane < 128 - turn, pltpu.roll(piece(first), 128 - turn, 1), pltpu.roll(piece(first + 1), 128 - turn, 1))

    def slice_tile(g):
        columns = []
        for t in range(9):
            value = window(t, 144 * g - 16 * t) if t < 8 else None
            if t > 0:
                before = window(t - 1, 144 * (g + 1) - 16 * t)
                value = before if value is None else jnp.where(lane < 16 * t, before, value)
            columns.append(value)
        tiles[g] = jnp.concatenate(columns, axis=0).astype(BF16)

    def tile_copy(to, origin):
        return pltpu.make_async_remote_copy(
            src_ref=tiles.at[to], dst_ref=out_ref.at[origin], send_sem=tile_send.at[to],
            recv_sem=tile_recv.at[origin], device_id=(to, sub), device_id_type=MESH)

    for half in range(2):
        fourth.finish(half)
        for part in range(2):
            stage_in(got3, half, part, spread.at[part])
        for i in halves[half]:
            second_back(i)
        for g in range(half * 8, half * 8 + 8):
            slice_tile(g)

        def tile_start(d, _):
            to = half * 8 + (group + d) % 8

            @pl.when(to != group)
            def _():
                tile_copy(to, group).start()

            return 0

        lax.fori_loop(0, 8, tile_start, 0)

    def tile_finish(d, _):
        other = (group + d) % GROUP
        tile_copy(other, group).wait_send()
        tile_copy(other, other).wait_recv()
        return 0

    own = pltpu.make_async_copy(tiles.at[group], out_ref.at[group], local_sem.at[10])
    own.start()
    own.wait()
    lax.fori_loop(1, GROUP, tile_finish, 0)


def forecast(ic, enc, spec, gain, up, down, proj):
    order, place = filter_tables()
    hbm = pl.BlockSpec(memory_space=pltpu.HBM)
    block = (SUB, 2, USED, 128)
    pair = (SUB, 2, 2, USED, 128)
    return pl.pallas_call(
        forecast_kernel,
        out_shape=jax.ShapeDtypeStruct((GROUP, 72, 128), BF16),
        in_specs=[hbm] * 10,
        out_specs=pl.BlockSpec(memory_space=pl.ANY),
        scratch_shapes=[
            pltpu.VMEM((BAND, 64, LONS), BF16), pltpu.VMEM((64, 128), BF16), pltpu.VMEM((2, 2, 128, 128), BF16),
            pltpu.VMEM((2, 128), F32), pltpu.VMEM((2, 256, 128), BF16), pltpu.VMEM((2, 128, 256), BF16),
            pltpu.VMEM((64, 128), BF16), pltpu.VMEM((384, LONS), BF16), pltpu.VMEM((8, 256), F32),
            pltpu.VMEM((BAND, 8, 256), F32),
            pltpu.VMEM((BAND, LATS, 256), BF16),
            pltpu.VMEM((128, 128), F32),
            pltpu.VMEM((2, 128, 128), BF16),
            pltpu.VMEM((2, ALL, 128), F32),
            pltpu.VMEM((2, ALL, 128), F32),
            pltpu.VMEM((BAND, LATS, 256), BF16),
            pltpu.VMEM(block, BF16), pltpu.VMEM(block, BF16), pltpu.VMEM(block, BF16), pltpu.VMEM(block, BF16),
            pltpu.VMEM(pair, BF16), pltpu.VMEM(pair, BF16), pltpu.VMEM(pair, BF16), pltpu.VMEM(pair, BF16),
            pltpu.VMEM((BAND, 128, LONS), BF16),
            pltpu.VMEM((18, 64, 128), F32),
            pltpu.VMEM((GROUP, 72, 128), BF16),
            pltpu.SemaphoreType.DMA((8, SUB)), pltpu.SemaphoreType.DMA((8, SUB)),
            pltpu.SemaphoreType.DMA((GROUP,)), pltpu.SemaphoreType.DMA((GROUP,)),
            pltpu.SemaphoreType.DMA((11,)),
        ],
        compiler_params=pltpu.CompilerParams(collective_id=0, has_side_effects=True, vmem_limit_bytes=62 << 20),
        name="forecast",
    )(jnp.transpose(ic, (1, 0, 2)), enc.T, spec, gain, up, down, proj, jnp.asarray(dft_table(), BF16), jnp.asarray(place), jnp.asarray(order))


def reduce_rows(pieces):
    rows = [[p[a:a + 1, :] for p in pieces] for a in range(8)]
    d = [[jnp.broadcast_to(rows[a][0][:, b:b + 1], (1, 128)) for b in range(8)] for a in range(8)]
    for a in range(8):
        inv = 1.0 / d[a][a]
        rows[a] = [x * inv for x in rows[a]]
        top = [None if b <= a else d[a][b] * inv for b in range(8)]
        d[a] = top
        for c in range(8):
            if c == a:
                continue
            f = d[c][a]
            rows[c] = [x - f * y for x, y in zip(rows[c], rows[a])]
            d[c] = [d[c][b] if b <= a else d[c][b] - f * top[b] for b in range(8)]
    return [jnp.concatenate([rows[a][l] for a in range(8)], axis=0) for l in range(len(pieces))]


def jordan(sys_ref, n, width):
    pieces = width // 128
    blocks = n // 8
    heads = n // 128
    def shift(vals, rows):
        lane = lax.broadcasted_iota(jnp.int32, (rows, 128), 1)
        r = [pltpu.roll(v, 120, 1) for v in vals[:heads]]
        if heads == 1:
            return r + list(vals[1:])
        return [jnp.where(lane < 120, r[h], r[(h + 1) % heads]) for h in range(heads)] + list(vals[heads:])
    def load(r):
        at = pl.ds(pl.multiple_of(r * 8, 8), 8)
        return [sys_ref[at, l * 128:(l + 1) * 128] for l in range(pieces)]
    def step(blk, red):
        nxt = lax.rem(blk + 1, blocks)
        x = load(nxt)
        c = [jnp.broadcast_to(x[0][:, b:b + 1], (8, 128)) for b in range(8)]
        for b in range(8):
            x = [v - c[b] * r[b:b + 1, :] for v, r in zip(x, red)]
        new = reduce_rows(shift(x, 8))
        left = sys_ref[:, 0:8]
        full = [sys_ref[:, l * 128:(l + 1) * 128] - dot(left, red[l], NN, EXACT) for l in range(pieces)]
        full = shift(full, n)
        for l in range(pieces):
            sys_ref[:, l * 128:(l + 1) * 128] = full[l]
        keep = shift(list(red), 8)
        at = pl.ds(pl.multiple_of(blk * 8, 8), 8)
        for l in range(pieces):
            sys_ref[at, l * 128:(l + 1) * 128] = keep[l]
        return tuple(new)
    lax.fori_loop(0, blocks, step, tuple(reduce_rows(load(0))))


def analysis_kernel(tile_ref, count_ref, pos_ref, val_ref, var_ref, mod_ref, out_ref, raw, state, pert, sysm, mtab):
    for q in range(16):
        raw[q * 72:(q + 1) * 72, :] = tile_ref[q].astype(F32)
    def collect(r, _):
        rows = raw[pl.ds(r, 16, stride=72), :]
        at = pl.ds(pl.multiple_of(r * 16, 16), 16)
        state[at, :] = rows
        mean = jnp.sum(rows, axis=0, keepdims=True) * (1.0 / 16)
        pert[at, :] = rows - mean
        return 0
    lax.fori_loop(0, 72, collect, 0, unroll=8)
    pos = pos_ref[...]
    col = pos >> 7
    lane = pos & 127
    u = jnp.floor((col.astype(F32) + 0.5) * (1.0 / 9)).astype(jnp.int32)
    row = (col - 9 * u) * 8 + u
    cell = pos - 144 * jnp.floor((pos.astype(F32) + 0.5) * (1.0 / 144)).astype(jnp.int32)
    pick = (lax.broadcasted_iota(jnp.int32, (128, 512), 0) == lane).astype(F32).astype(BF16)
    pick_cell = (lax.broadcasted_iota(jnp.int32, (144, 512), 0) == cell).astype(F32).astype(BF16)
    def gather(i, acc):
        at = pl.ds(pl.multiple_of(i * 128, 128), 128)
        part = dot(state[at, :].astype(BF16), pick, NN)
        for k in range(8):
            acc = acc + jnp.where(row == i * 8 + k, part[k * 16:(k + 1) * 16, :], 0.0)
        return acc
    picked = lax.fori_loop(0, 9, gather, jnp.zeros((16, 512), F32))
    mod = mod_ref[...]
    hi = mod.astype(BF16)
    rest = mod - hi.astype(F32)
    mid = rest.astype(BF16)
    low = (rest - mid.astype(F32)).astype(BF16)
    mod_at = dot(hi, pick_cell, NN) + dot(mid, pick_cell, NN) + dot(low, pick_cell, NN)
    valid = lax.broadcasted_iota(jnp.int32, (1, 512), 1) < count_ref[0, 0]
    root = jnp.where(valid, lax.rsqrt(var_ref[...]), 0.0)
    dev = (picked - jnp.sum(picked, axis=0, keepdims=True) * (1.0 / 16)) * (root * (1.0 / math.sqrt(15.0)))
    innov = jnp.where(valid, val_ref[...] - picked, 0.0) * root
    anom = jnp.concatenate([dev[k:k + 1, :] * mod_at for k in range(16)], axis=0)
    eye = (lax.broadcasted_iota(jnp.int32, (256, 256), 0) == lax.broadcasted_iota(jnp.int32, (256, 256), 1)).astype(F32)
    sysm[:, 0:256] = dot(anom, anom, NT, EXACT) + eye
    rhs = jnp.concatenate([innov, jnp.zeros((112, 512), F32)], axis=0)
    sysm[:, 256:384] = dot(anom, rhs, NT, EXACT)
    jordan(sysm, 256, 384)
    wt = sysm[:, 256:384].T[0:16, :]
    spread = jnp.concatenate([wt] * 16, axis=0)
    same = (lax.broadcasted_iota(jnp.int32, (256, 256), 0) // 16) == (lax.broadcasted_iota(jnp.int32, (256, 256), 1) // 16)
    spread = jnp.where(same, spread, 0.0)
    modk = jnp.concatenate([mod * (1.0 / math.sqrt(15.0))] * 16, axis=0)
    coef = dot(spread, modk, NN, EXACT)
    for t in range(9):
        start = (128 * t) % 144
        if start + 128 <= 144:
            part = coef[:, start:start + 128]
        else:
            part = jnp.concatenate([coef[:, start:144], coef[:, 0:start - 16]], axis=1)
        mtab[t] = part
    def apply(t, _):
        for u8 in range(8):
            at = pl.multiple_of((t * 8 + u8) * 16, 16)
            acc = state[pl.ds(at, 16), :]
            p = pert[pl.ds(at, 16), :]
            for k in range(16):
                acc = acc + mtab[t, k * 16:(k + 1) * 16, :] * p[k:k + 1, :]
            out_ref[:, pl.ds(pl.multiple_of((9 * u8 + t) * 128, 128), 128)] = acc.astype(BF16)
        return 0
    lax.fori_loop(0, 9, apply, 0)


def analysis(tile, count, pos, val, var, mod):
    v = pl.BlockSpec(memory_space=pltpu.VMEM)
    return pl.pallas_call(
        analysis_kernel,
        out_shape=jax.ShapeDtypeStruct((16, 9216), BF16),
        in_specs=[v, pl.BlockSpec(memory_space=pltpu.SMEM), v, v, v, v],
        out_specs=v,
        scratch_shapes=[pltpu.VMEM((1152, 128), F32), pltpu.VMEM((1152, 128), F32), pltpu.VMEM((1152, 128), F32),
                        pltpu.VMEM((256, 384), F32), pltpu.VMEM((9, 256, 128), F32)],
        compiler_params=pltpu.CompilerParams(vmem_limit_bytes=48 << 20),
        name="analysis",
    )(tile, count, pos, val, var, mod)


def shards(ic, enc, spec, gain, up, down, proj, pos, count, value, var, mod):
    tile = forecast(ic[0], enc, spec, gain, up, down, proj)
    out = analysis(tile, count, pos[0], value[0], var[0], mod[0, 0])
    return out[None, None]


def solution(mesh):
    part = P("sub", "group", None)
    return jax.shard_map(
        shards,
        mesh=mesh,
        in_specs=(P("group", None, "sub", None),) + (P(),) * 6
        + (part, P("sub", "group"), part, part, P("sub", "group", None, None)),
        out_specs=P("sub", "group", None, None),
        check_vma=False,
    )
```

```python
import functools
import math

import jax
import jax.numpy as jnp
import numpy as np
from jax import lax
from jax.experimental import pallas as pl
from jax.experimental.pallas import tpu as pltpu
from jax.sharding import PartitionSpec as P

F32 = jnp.float32
BF16 = jnp.bfloat16
EXACT = lax.Precision.HIGHEST
MESH = pl.DeviceIdType.MESH
NN = ((1,), (0,))
NT = ((1,), (1,))

LATS = 192
LONS = 384
DEGREES = 192
SUB = 32
GROUP = 16
BAND = 6
HALF = BAND // 2
USED = HALF * BAND
GAP = 24
ROWS = 2 * GAP
ALL = SUB * ROWS


def dot(a, b, dims, precision=None):
    return lax.dot_general(a, b, (dims, ((), ())), precision=precision, preferred_element_type=F32)


def dft_table():
    m = (BAND * np.arange(SUB)[None, :] + np.arange(BAND)[:, None]).reshape(-1)
    angle = 2.0 * np.pi * ((m[:, None] * np.arange(LONS)[None, :]) % LONS) / LONS
    return np.concatenate([np.cos(angle), -np.sin(angle)], axis=0)


def filter_tables():
    colatitude = (np.arange(LATS) + 0.5) * np.pi / LATS
    x, sine = np.cos(colatitude), np.sin(colatitude)
    m = np.arange(LATS, dtype=np.float64)[:, None]
    gammas = np.array([math.lgamma(v + 0.5) - math.lgamma(v + 1.0) for v in range(LATS)])[:, None]
    start = np.exp(
        0.5 * (np.log((2 * m + 1) / (4 * np.pi)) + gammas - 0.5 * np.log(np.pi)) + m * np.log(sine)[None, :]
    )
    earlier, previous, squares = np.zeros_like(start), np.zeros_like(start), np.zeros_like(start)
    for l in range(DEGREES + 1):
        up = np.sqrt((4.0 * l * l - 1.0) / np.maximum(l * l - m * m, 1.0)) if l else 0.0 * m
        low = np.sqrt(np.maximum((l - 1.0) ** 2 - m * m, 0.0) / max(4.0 * (l - 1.0) ** 2 - 1.0, 1.0))
        value = up * (x[None, :] * previous - low * earlier)
        value = np.where(l == m + 1, x[None, :] * np.sqrt(2 * m + 3) * start, value)
        value = np.where(l == m, start, np.where(l < m, 0.0, value))
        earlier, previous = previous, value
        if l < DEGREES:
            squares += value * value
    weight = 2.0 * np.pi * (np.pi / LATS) * sine[None, :] * np.where(m == 0, 1.0, 2.0) / LONS
    e = np.sqrt((DEGREES**2 - m * m) / (4.0 * DEGREES**2 - 1.0))
    per_order = [previous * e * weight, earlier * e * weight, squares * weight, previous, earlier]
    order = np.zeros((SUB, BAND, 8, 256), np.float32)
    place = np.zeros((8, 256), np.float32)
    place[0] = 2.0 + np.arange(256)
    lats = (BAND * np.arange(SUB)[None, :] + np.arange(BAND)[:, None]).reshape(-1)
    for k, table in enumerate(per_order):
        order[:, :, k, :LATS] = table.reshape(SUB, BAND, LATS)[:, :, lats]
    place[0, :LATS] = x[lats].astype(np.float32)
    place[1, :LATS] = x[lats] - x[lats].astype(np.float32).astype(np.float64)
    place[2] = np.arange(256)
    return order, place


def erf_gelu(x):
    return 0.5 * x * (1.0 + lax.erf(x * (1.0 / math.sqrt(2.0))))


def forecast_kernel(
    ic_hbm, enc_hbm, spec_hbm, gain_hbm, up_hbm, down_hbm, proj_hbm, dft_hbm, place_hbm, order_hbm, out_ref,
    fields, enc_ref, spec_ref, gain_ref, up_ref, down_ref, proj_ref, dft_ref, place_ref, order_ref,
    filt, gain, mix, spread, result, source, sent0, got0, sent1, got1, sent2, got2, sent3, got3,
    hidden, cast, tiles, send_sem, recv_sem, tile_send, tile_recv, local_sem,
):
    group = lax.axis_index("group")
    sub = lax.axis_index("sub")

    barrier = pltpu.get_barrier_semaphore()

    def greet_subs(d, _):
        pl.semaphore_signal(barrier, inc=1, device_id=(group, (sub + d) % SUB), device_id_type=MESH)
        return 0

    def greet_tiles(d, _):
        pl.semaphore_signal(barrier, inc=1, device_id=((group + d) % GROUP, sub), device_id_type=MESH)
        return 0

    lax.fori_loop(1, SUB, greet_subs, 0)
    lax.fori_loop(1, GROUP, greet_tiles, 0)

    loads = {}
    for n, (name, src, dst) in enumerate((
        ("fields", ic_hbm, fields), ("dft", dft_hbm, dft_ref), ("order", order_hbm.at[sub], order_ref),
        ("place", place_hbm, place_ref), ("enc", enc_hbm, enc_ref), ("spec", spec_hbm, spec_ref),
        ("gain", gain_hbm, gain_ref), ("up", up_hbm, up_ref), ("down", down_hbm, down_ref),
        ("proj", proj_hbm, proj_ref),
    )):
        loads[name] = pltpu.make_async_copy(src, dst, local_sem.at[n])
        loads[name].start()

    def far_first(e):
        k = (e // 2) % 8
        z = (sub // 4 + 4 + (k // 2) * (1 - 2 * (k % 2)) - k % 2) % 8
        return z * 4 + (sub // 2 + 1 - e // 16) % 2 * 2 + (sub + 1 + e) % 2

    class Exchange:
        def __init__(self, stage, sent, got):
            self.stage, self.sent, self.got = stage, sent, got

        def copy(self, half, d):
            band = far_first(d)
            return pltpu.make_async_remote_copy(
                src_ref=self.sent.at[band, half], dst_ref=self.got.at[sub, half],
                send_sem=send_sem.at[self.stage * 2 + half, d], recv_sem=recv_sem.at[self.stage * 2 + half, d],
                device_id=(group, band), device_id_type=MESH)

        def start(self, half):
            def body(d, _):
                self.copy(half, d).start()
                return 0

            lax.fori_loop(0, SUB - 1, body, 0)
            self.got[sub, half] = self.sent[sub, half]

        def finish(self, half):
            def body(d, _):
                self.copy(half, d).wait()
                return 0

            lax.fori_loop(0, SUB - 1, body, 0)

    def row_of(i, mm):
        return (i // HALF) * GAP + (i % HALF) * BAND + mm

    def put(dest, i, mm, rows):
        dest[pl.ds(row_of(i, mm), SUB, stride=ROWS), :] = rows

    def take(src, i, mm):
        return src[pl.ds(row_of(i, mm), SUB, stride=ROWS), :]

    def stage_out(src, sent, half, part):
        def body(d, _):
            block = src[pl.ds(pl.multiple_of(d * ROWS + half * GAP, 8), USED), :].astype(BF16)
            if part is None:
                sent[d, half] = block
            else:
                sent[d, half, part] = block
            return 0
        lax.fori_loop(0, SUB, body, 0, unroll=8)

    def stage_in(got, half, part, dest):
        def body(d, _):
            block = got[d, half] if part is None else got[d, half, part]
            dest[pl.ds(pl.multiple_of(d * ROWS + half * GAP, 8), USED), :] = block.astype(F32)
            return 0
        lax.fori_loop(0, SUB, body, 0, unroll=8)

    halves = [range(0, HALF), range(HALF, BAND)]
    first, second = Exchange(0, sent0, got0), Exchange(1, sent1, got1)
    third, fourth = Exchange(2, sent2, got2), Exchange(3, sent3, got3)
    empty = jnp.zeros((64, LONS), BF16)
    loads["fields"].wait()
    loads["dft"].wait()
    for half in range(2):
        for i in halves[half]:
            here = fields[i]
            real = jnp.concatenate([here, empty], axis=0)
            imag = jnp.concatenate([empty, here], axis=0)
            zonal = dot(dft_ref[0:192, :], real, NT) + dot(dft_ref[192:384, :], imag, NT)
            for mm in range(BAND):
                put(spread.at[0], i, mm, zonal[mm * SUB:(mm + 1) * SUB, :])
        stage_out(spread.at[0], sent0, half, None)
        if half == 0:
            pl.semaphore_wait(barrier, SUB + GROUP - 2)
        first.start(half)

    loads["order"].wait()
    loads["place"].wait()
    for mm in range(BAND):
        rows = order_ref[mm]
        col = jnp.concatenate([rows, place_ref[...], jnp.zeros((112, 256), F32)], axis=0).T[0:LATS, :]
        for b in range(4):
            c = col[b * 48:(b + 1) * 48, :]
            top = c[:, 3:4] * rows[1:2, :] - c[:, 4:5] * rows[0:1, :]
            gap = (c[:, 8:9] - place_ref[0:1, :]) + (c[:, 9:10] - place_ref[1:2, :])
            same = c[:, 10:11] == place_ref[2:3, :]
            value = jnp.where(same, rows[2:3, :], top / jnp.where(same, 1.0, gap))
            filt[mm, b * 48:(b + 1) * 48, :] = value.astype(BF16)
    for name in ("enc", "spec", "gain", "up", "down", "proj"):
        loads[name].wait()
    gain[...] = jnp.concatenate([gain_ref[...], jnp.zeros((126, 128), F32)], axis=0).T
    enc = enc_ref[...].T
    none = jnp.zeros((128, 64), BF16)
    enc_real = jnp.concatenate([enc, none], axis=1)
    enc_imag = jnp.concatenate([none, enc], axis=1)
    mix[0] = (dot(spec_ref[0, 0], enc_real, NN) - dot(spec_ref[0, 1], enc_imag, NN)).astype(BF16)
    mix[1] = (dot(spec_ref[0, 1], enc_real, NN) + dot(spec_ref[0, 0], enc_imag, NN)).astype(BF16)

    def latitude(i, part):
        return jnp.concatenate([take(spread.at[part], i, mm) for mm in range(BAND)], axis=0).astype(BF16)

    def apply_filter(parts, sent, exchange):
        for mm in range(BAND):
            for part in range(parts):
                source[mm, :, part * 128:(part + 1) * 128] = jnp.concatenate(
                    [take(spread.at[part], i, mm) for i in range(BAND)], axis=0).astype(BF16)
        for half in range(2):
            for mm in range(BAND):
                filtered = dot(filt[mm, half * 96:(half + 1) * 96, 0:LATS], source[mm, :, 0:parts * 128], NN)
                for part in range(parts):
                    for k, i in enumerate(halves[half]):
                        put(result.at[part], i, mm, filtered[k * SUB:(k + 1) * SUB, part * 128:(part + 1) * 128])
            for part in range(parts):
                stage_out(result.at[part], sent, half, part if parts > 1 else None)
            exchange.start(half)

    for half in range(2):
        first.finish(half)
        stage_in(got0, half, None, spread.at[0])
    apply_filter(1, sent1, second)

    def pointwise(layer, summed):
        centred = summed - jnp.mean(summed, axis=0, keepdims=True)
        spread_of = jnp.mean(centred * centred, axis=0, keepdims=True)
        normed = (centred * lax.rsqrt(spread_of + 1e-05) * gain[:, layer:layer + 1]).astype(BF16)
        lifted = erf_gelu(dot(up_ref[layer], normed, NN)).astype(BF16)
        return (summed + dot(down_ref[layer], lifted, NN)).astype(BF16)

    for half in range(2):
        second.finish(half)
        stage_in(got1, half, None, spread.at[0])
        for i in halves[half]:
            back = latitude(i, 0)
            real = dot(mix[0], back, NT).astype(BF16)
            imag = dot(mix[1], back, NT).astype(BF16)
            summed = dot(enc, fields[i], NN)
            summed = summed + dot(real, dft_ref[0:192, :], NN) + dot(imag, dft_ref[192:384, :], NN)
            after = pointwise(0, summed)
            hidden[i] = after
            zonal = dot(dft_ref[...], after, NT)
            for part in range(2):
                for mm in range(BAND):
                    at = part * 192 + mm * SUB
                    put(result.at[part], i, mm, zonal[at:at + SUB, :])
        for part in range(2):
            stage_out(result.at[part], sent2, half, part)
        third.start(half)

    for half in range(2):
        third.finish(half)
        for part in range(2):
            stage_in(got2, half, part, spread.at[part])
    apply_filter(2, sent3, fourth)

    def second_back(i):
        back_real = latitude(i, 0)
        back_imag = latitude(i, 1)
        w_real, w_imag = spec_ref[1, 0], spec_ref[1, 1]
        real = (dot(w_real, back_real, NT) - dot(w_imag, back_imag, NT)).astype(BF16)
        imag = (dot(w_imag, back_real, NT) + dot(w_real, back_imag, NT)).astype(BF16)
        summed = hidden[i].astype(F32)
        summed = summed + dot(real, dft_ref[0:192, :], NN) + dot(imag, dft_ref[192:384, :], NN)
        ahead = fields[i].astype(F32) + dot(proj_ref[...], pointwise(1, summed), NN)
        for l in range(3):
            cast[3 * i + l] = ahead[:, l * 128:(l + 1) * 128]

    lane = lax.broadcasted_iota(jnp.int32, (8, 128), 1)

    def window(w, begin):
        first, turn = begin // 128, begin % 128
        def piece(j):
            return cast[min(max(j, 0), 17), pl.ds(w, 8, stride=8), :]
        if turn == 0:
            return piece(first)
        return jnp.where(
            lane < 128 - turn, pltpu.roll(piece(first), 128 - turn, 1), pltpu.roll(piece(first + 1), 128 - turn, 1))

    def slice_tile(g):
        columns = []
        for t in range(9):
            value = window(t, 144 * g - 16 * t) if t < 8 else None
            if t > 0:
                before = window(t - 1, 144 * (g + 1) - 16 * t)
                value = before if value is None else jnp.where(lane < 16 * t, before, value)
            columns.append(value)
        tiles[g] = jnp.concatenate(columns, axis=0).astype(BF16)

    def tile_copy(to, origin):
        return pltpu.make_async_remote_copy(
            src_ref=tiles.at[to], dst_ref=out_ref.at[origin], send_sem=tile_send.at[to],
            recv_sem=tile_recv.at[origin], device_id=(to, sub), device_id_type=MESH)

    for half in range(2):
        fourth.finish(half)
        for part in range(2):
            stage_in(got3, half, part, spread.at[part])
        for i in halves[half]:
            second_back(i)
        for g in range(half * 8, half * 8 + 8):
            slice_tile(g)

        def tile_start(d, _):
            to = half * 8 + (group + d) % 8

            @pl.when(to != group)
            def _():
                tile_copy(to, group).start()

            return 0

        lax.fori_loop(0, 8, tile_start, 0)

    def tile_finish(d, _):
        other = (group + d) % GROUP
        tile_copy(other, group).wait_send()
        tile_copy(other, other).wait_recv()
        return 0

    own = pltpu.make_async_copy(tiles.at[group], out_ref.at[group], local_sem.at[10])
    own.start()
    own.wait()
    lax.fori_loop(1, GROUP, tile_finish, 0)


def forecast(ic, enc, spec, gain, up, down, proj):
    order, place = filter_tables()
    hbm = pl.BlockSpec(memory_space=pltpu.HBM)
    block = (SUB, 2, USED, 128)
    pair = (SUB, 2, 2, USED, 128)
    return pl.pallas_call(
        forecast_kernel,
        out_shape=jax.ShapeDtypeStruct((GROUP, 72, 128), BF16),
        in_specs=[hbm] * 10,
        out_specs=pl.BlockSpec(memory_space=pl.ANY),
        scratch_shapes=[
            pltpu.VMEM((BAND, 64, LONS), BF16), pltpu.VMEM((64, 128), BF16), pltpu.VMEM((2, 2, 128, 128), BF16),
            pltpu.VMEM((2, 128), F32), pltpu.VMEM((2, 256, 128), BF16), pltpu.VMEM((2, 128, 256), BF16),
            pltpu.VMEM((64, 128), BF16), pltpu.VMEM((384, LONS), BF16), pltpu.VMEM((8, 256), F32),
            pltpu.VMEM((BAND, 8, 256), F32),
            pltpu.VMEM((BAND, LATS, 256), BF16),
            pltpu.VMEM((128, 128), F32),
            pltpu.VMEM((2, 128, 128), BF16),
            pltpu.VMEM((2, ALL, 128), F32),
            pltpu.VMEM((2, ALL, 128), F32),
            pltpu.VMEM((BAND, LATS, 256), BF16),
            pltpu.VMEM(block, BF16), pltpu.VMEM(block, BF16), pltpu.VMEM(block, BF16), pltpu.VMEM(block, BF16),
            pltpu.VMEM(pair, BF16), pltpu.VMEM(pair, BF16), pltpu.VMEM(pair, BF16), pltpu.VMEM(pair, BF16),
            pltpu.VMEM((BAND, 128, LONS), BF16),
            pltpu.VMEM((18, 64, 128), F32),
            pltpu.VMEM((GROUP, 72, 128), BF16),
            pltpu.SemaphoreType.DMA((8, SUB)), pltpu.SemaphoreType.DMA((8, SUB)),
            pltpu.SemaphoreType.DMA((GROUP,)), pltpu.SemaphoreType.DMA((GROUP,)),
            pltpu.SemaphoreType.DMA((11,)),
        ],
        compiler_params=pltpu.CompilerParams(collective_id=0, has_side_effects=True, vmem_limit_bytes=62 << 20),
        name="forecast",
    )(jnp.transpose(ic, (1, 0, 2)), enc.T, spec, gain, up, down, proj, jnp.asarray(dft_table(), BF16), jnp.asarray(place), jnp.asarray(order))


def reduce_rows(rows, at):
    lines = [rows[a:a + 1, :] for a in range(8)]
    d = [[jnp.broadcast_to(lines[a][:, at + b:at + b + 1], (1, 128)) for b in range(8)] for a in range(8)]
    for a in range(8):
        inv = 1.0 / d[a][a]
        lines[a] = lines[a] * inv
        top = [None if b <= a else d[a][b] * inv for b in range(8)]
        d[a] = top
        for c in range(8):
            if c == a:
                continue
            f = d[c][a]
            lines[c] = lines[c] - f * lines[a]
            d[c] = [d[c][b] if b <= a else d[c][b] - f * top[b] for b in range(8)]
    return lines


def inverse(block):
    lane = lax.broadcasted_iota(jnp.int32, (64, 128), 1)
    row = lax.broadcasted_iota(jnp.int32, (64, 128), 0)
    both = jnp.where(lane < 64, block, (lane - 64 == row).astype(F32))
    parts = [both[r * 8:(r + 1) * 8, :] for r in range(8)]
    for step in range(8):
        at = step * 8
        lines = reduce_rows(parts[step], at)
        for r in range(8):
            if r == step:
                continue
            x = parts[r]
            c = [jnp.broadcast_to(x[:, at + b:at + b + 1], (8, 128)) for b in range(8)]
            terms = [c[b] * lines[b] for b in range(8)]
            parts[r] = x - (((terms[0] + terms[1]) + (terms[2] + terms[3]))
                            + ((terms[4] + terms[5]) + (terms[6] + terms[7])))
        parts[step] = jnp.concatenate(lines, axis=0)
    return jnp.concatenate(parts, axis=0)[:, 64:128]


def jordan(sys_ref):
    def shifted(left, right, rows):
        lane = lax.broadcasted_iota(jnp.int32, (rows, 128), 1)
        left, right = pltpu.roll(left, 64, 1), pltpu.roll(right, 64, 1)
        return jnp.where(lane < 64, left, right), jnp.where(lane < 64, right, left)

    def step(blk, _):
        at = pl.ds(pl.multiple_of(blk * 64, 64), 64)
        inv = inverse(sys_ref[at, 0:128])
        rows = dot(inv, sys_ref[at, :], NN, EXACT)
        full = sys_ref[...] - dot(sys_ref[:, 0:64], rows, NN, EXACT)
        sys_ref[:, 256:384] = full[:, 256:384]
        sys_ref[:, 0:128], sys_ref[:, 128:256] = shifted(full[:, 0:128], full[:, 128:256], 256)
        sys_ref[at, 256:384] = rows[:, 256:384]
        sys_ref[at, 0:128], sys_ref[at, 128:256] = shifted(rows[:, 0:128], rows[:, 128:256], 64)
        return 0

    lax.fori_loop(0, 4, step, 0)


def analysis_kernel(tile_ref, count_ref, pos_ref, val_ref, var_ref, mod_ref, out_ref, raw, state, pert, sysm, mtab):
    for q in range(16):
        raw[q * 72:(q + 1) * 72, :] = tile_ref[q].astype(F32)
    def collect(r, _):
        rows = raw[pl.ds(r, 16, stride=72), :]
        at = pl.ds(pl.multiple_of(r * 16, 16), 16)
        state[at, :] = rows
        mean = jnp.sum(rows, axis=0, keepdims=True) * (1.0 / 16)
        pert[at, :] = rows - mean
        return 0
    lax.fori_loop(0, 72, collect, 0, unroll=8)
    pos = pos_ref[...]
    col = pos >> 7
    lane = pos & 127
    u = jnp.floor((col.astype(F32) + 0.5) * (1.0 / 9)).astype(jnp.int32)
    row = (col - 9 * u) * 8 + u
    cell = pos - 144 * jnp.floor((pos.astype(F32) + 0.5) * (1.0 / 144)).astype(jnp.int32)
    pick = (lax.broadcasted_iota(jnp.int32, (128, 512), 0) == lane).astype(F32).astype(BF16)
    pick_cell = (lax.broadcasted_iota(jnp.int32, (144, 512), 0) == cell).astype(F32).astype(BF16)
    def gather(i, acc):
        at = pl.ds(pl.multiple_of(i * 128, 128), 128)
        part = dot(state[at, :].astype(BF16), pick, NN)
        for k in range(8):
            acc = acc + jnp.where(row == i * 8 + k, part[k * 16:(k + 1) * 16, :], 0.0)
        return acc
    picked = lax.fori_loop(0, 9, gather, jnp.zeros((16, 512), F32))
    mod = mod_ref[...]
    hi = mod.astype(BF16)
    rest = mod - hi.astype(F32)
    mid = rest.astype(BF16)
    low = (rest - mid.astype(F32)).astype(BF16)
    mod_at = dot(hi, pick_cell, NN) + dot(mid, pick_cell, NN) + dot(low, pick_cell, NN)
    valid = lax.broadcasted_iota(jnp.int32, (1, 512), 1) < count_ref[0, 0]
    root = jnp.where(valid, lax.rsqrt(var_ref[...]), 0.0)
    dev = (picked - jnp.sum(picked, axis=0, keepdims=True) * (1.0 / 16)) * (root * (1.0 / math.sqrt(15.0)))
    innov = jnp.where(valid, val_ref[...] - picked, 0.0) * root
    anom = jnp.concatenate([dev[k:k + 1, :] * mod_at for k in range(16)], axis=0)
    eye = (lax.broadcasted_iota(jnp.int32, (256, 256), 0) == lax.broadcasted_iota(jnp.int32, (256, 256), 1)).astype(F32)
    sysm[:, 0:256] = dot(anom, anom, NT, EXACT) + eye
    rhs = jnp.concatenate([innov, jnp.zeros((112, 512), F32)], axis=0)
    sysm[:, 256:384] = dot(anom, rhs, NT, EXACT)
    jordan(sysm)
    wt = sysm[:, 256:384].T[0:16, :]
    spread = jnp.concatenate([wt] * 16, axis=0)
    same = (lax.broadcasted_iota(jnp.int32, (256, 256), 0) // 16) == (lax.broadcasted_iota(jnp.int32, (256, 256), 1) // 16)
    spread = jnp.where(same, spread, 0.0)
    modk = jnp.concatenate([mod * (1.0 / math.sqrt(15.0))] * 16, axis=0)
    coef = dot(spread, modk, NN, EXACT)
    for t in range(9):
        start = (128 * t) % 144
        if start + 128 <= 144:
            part = coef[:, start:start + 128]
        else:
            part = jnp.concatenate([coef[:, start:144], coef[:, 0:start - 16]], axis=1)
        mtab[t] = part
    def apply(t, _):
        for u8 in range(8):
            at = pl.multiple_of((t * 8 + u8) * 16, 16)
            acc = state[pl.ds(at, 16), :]
            p = pert[pl.ds(at, 16), :]
            for k in range(16):
                acc = acc + mtab[t, k * 16:(k + 1) * 16, :] * p[k:k + 1, :]
            out_ref[:, pl.ds(pl.multiple_of((9 * u8 + t) * 128, 128), 128)] = acc.astype(BF16)
        return 0
    lax.fori_loop(0, 9, apply, 0)


def analysis(tile, count, pos, val, var, mod):
    v = pl.BlockSpec(memory_space=pltpu.VMEM)
    return pl.pallas_call(
        analysis_kernel,
        out_shape=jax.ShapeDtypeStruct((16, 9216), BF16),
        in_specs=[v, pl.BlockSpec(memory_space=pltpu.SMEM), v, v, v, v],
        out_specs=v,
        scratch_shapes=[pltpu.VMEM((1152, 128), F32), pltpu.VMEM((1152, 128), F32), pltpu.VMEM((1152, 128), F32),
                        pltpu.VMEM((256, 384), F32), pltpu.VMEM((9, 256, 128), F32)],
        compiler_params=pltpu.CompilerParams(vmem_limit_bytes=48 << 20),
        name="analysis",
    )(tile, count, pos, val, var, mod)


def shards(ic, enc, spec, gain, up, down, proj, pos, count, value, var, mod):
    tile = forecast(ic[0], enc, spec, gain, up, down, proj)
    out = analysis(tile, count, pos[0], value[0], var[0], mod[0, 0])
    return out[None, None]


def solution(mesh):
    part = P("sub", "group", None)
    return jax.shard_map(
        shards,
        mesh=mesh,
        in_specs=(P("group", None, "sub", None),) + (P(),) * 6
        + (part, P("sub", "group"), part, part, P("sub", "group", None, None)),
        out_specs=P("sub", "group", None, None),
        check_vma=False,
    )
```

```python
import functools
import math

import jax
import jax.numpy as jnp
import numpy as np
from jax import lax
from jax.experimental import pallas as pl
from jax.experimental.pallas import tpu as pltpu
from jax.sharding import PartitionSpec as P

F32 = jnp.float32
BF16 = jnp.bfloat16
EXACT = lax.Precision.HIGHEST
MESH = pl.DeviceIdType.MESH
NN = ((1,), (0,))
NT = ((1,), (1,))

LATS = 192
LONS = 384
DEGREES = 192
SUB = 32
GROUP = 16
BAND = 6
HALF = BAND // 2
USED = HALF * BAND
GAP = 24
ROWS = 2 * GAP
ALL = SUB * ROWS


def dot(a, b, dims, precision=None):
    return lax.dot_general(a, b, (dims, ((), ())), precision=precision, preferred_element_type=F32)


def dft_table():
    m = (BAND * np.arange(SUB)[None, :] + np.arange(BAND)[:, None]).reshape(-1)
    angle = 2.0 * np.pi * ((m[:, None] * np.arange(LONS)[None, :]) % LONS) / LONS
    return np.concatenate([np.cos(angle), -np.sin(angle)], axis=0)


def filter_tables():
    colatitude = (np.arange(LATS) + 0.5) * np.pi / LATS
    x, sine = np.cos(colatitude), np.sin(colatitude)
    m = np.arange(LATS, dtype=np.float64)[:, None]
    gammas = np.array([math.lgamma(v + 0.5) - math.lgamma(v + 1.0) for v in range(LATS)])[:, None]
    start = np.exp(
        0.5 * (np.log((2 * m + 1) / (4 * np.pi)) + gammas - 0.5 * np.log(np.pi)) + m * np.log(sine)[None, :]
    )
    earlier, previous, squares = np.zeros_like(start), np.zeros_like(start), np.zeros_like(start)
    for l in range(DEGREES + 1):
        up = np.sqrt((4.0 * l * l - 1.0) / np.maximum(l * l - m * m, 1.0)) if l else 0.0 * m
        low = np.sqrt(np.maximum((l - 1.0) ** 2 - m * m, 0.0) / max(4.0 * (l - 1.0) ** 2 - 1.0, 1.0))
        value = up * (x[None, :] * previous - low * earlier)
        value = np.where(l == m + 1, x[None, :] * np.sqrt(2 * m + 3) * start, value)
        value = np.where(l == m, start, np.where(l < m, 0.0, value))
        earlier, previous = previous, value
        if l < DEGREES:
            squares += value * value
    weight = 2.0 * np.pi * (np.pi / LATS) * sine[None, :] * np.where(m == 0, 1.0, 2.0) / LONS
    e = np.sqrt((DEGREES**2 - m * m) / (4.0 * DEGREES**2 - 1.0))
    per_order = [previous * e * weight, earlier * e * weight, squares * weight, previous, earlier]
    order = np.zeros((SUB, BAND, 8, 256), np.float32)
    place = np.zeros((8, 256), np.float32)
    place[0] = 2.0 + np.arange(256)
    lats = (BAND * np.arange(SUB)[None, :] + np.arange(BAND)[:, None]).reshape(-1)
    for k, table in enumerate(per_order):
        order[:, :, k, :LATS] = table.reshape(SUB, BAND, LATS)[:, :, lats]
    place[0, :LATS] = x[lats].astype(np.float32)
    place[1, :LATS] = x[lats] - x[lats].astype(np.float32).astype(np.float64)
    place[2] = np.arange(256)
    return order, place


def erf_gelu(x):
    return 0.5 * x * (1.0 + lax.erf(x * (1.0 / math.sqrt(2.0))))


def forecast_kernel(
    ic_hbm, enc_hbm, spec_hbm, gain_hbm, up_hbm, down_hbm, proj_hbm, dft_hbm, place_hbm, order_hbm, out_ref,
    fields, enc_ref, spec_ref, gain_ref, up_ref, down_ref, proj_ref, dft_ref, place_ref, order_ref,
    filt, gain, mix, spread, result, source, sent0, got0, sent1, got1, sent2, got2, sent3, got3,
    hidden, cast, tiles, send_sem, recv_sem, tile_send, tile_recv, local_sem,
):
    group = lax.axis_index("group")
    sub = lax.axis_index("sub")

    barrier = pltpu.get_barrier_semaphore()

    def greet_subs(d, _):
        pl.semaphore_signal(barrier, inc=1, device_id=(group, (sub + d) % SUB), device_id_type=MESH)
        return 0

    def greet_tiles(d, _):
        pl.semaphore_signal(barrier, inc=1, device_id=((group + d) % GROUP, sub), device_id_type=MESH)
        return 0

    lax.fori_loop(1, SUB, greet_subs, 0)
    lax.fori_loop(1, GROUP, greet_tiles, 0)

    loads = {}
    for n, (name, src, dst) in enumerate((
        ("fields", ic_hbm, fields), ("dft", dft_hbm, dft_ref), ("order", order_hbm.at[sub], order_ref),
        ("place", place_hbm, place_ref), ("enc", enc_hbm, enc_ref), ("spec", spec_hbm, spec_ref),
        ("gain", gain_hbm, gain_ref), ("up", up_hbm, up_ref), ("down", down_hbm, down_ref),
        ("proj", proj_hbm, proj_ref),
    )):
        loads[name] = pltpu.make_async_copy(src, dst, local_sem.at[n])
        loads[name].start()

    def far_first(e):
        k = (e // 2) % 8
        z = (sub // 4 + 4 + (k // 2) * (1 - 2 * (k % 2)) - k % 2) % 8
        return z * 4 + (sub // 2 + 1 - e // 16) % 2 * 2 + (sub + 1 + e) % 2

    class Exchange:
        def __init__(self, stage, sent, got):
            self.stage, self.sent, self.got = stage, sent, got

        def copy(self, half, d):
            band = far_first(d)
            return pltpu.make_async_remote_copy(
                src_ref=self.sent.at[band, half], dst_ref=self.got.at[sub, half],
                send_sem=send_sem.at[self.stage * 2 + half, d], recv_sem=recv_sem.at[self.stage * 2 + half, d],
                device_id=(group, band), device_id_type=MESH)

        def start(self, half):
            def body(d, _):
                self.copy(half, d).start()
                return 0

            lax.fori_loop(0, SUB - 1, body, 0)
            self.got[sub, half] = self.sent[sub, half]

        def finish(self, half):
            def body(d, _):
                self.copy(half, d).wait()
                return 0

            lax.fori_loop(0, SUB - 1, body, 0)

    def row_of(i, mm):
        return (i // HALF) * GAP + (i % HALF) * BAND + mm

    def put(dest, i, mm, rows):
        dest[pl.ds(row_of(i, mm), SUB, stride=ROWS), :] = rows

    def take(src, i, mm):
        return src[pl.ds(row_of(i, mm), SUB, stride=ROWS), :]

    def stage_out(src, sent, half, part):
        def body(d, _):
            block = src[pl.ds(pl.multiple_of(d * ROWS + half * GAP, 8), USED), :].astype(BF16)
            if part is None:
                sent[d, half] = block
            else:
                sent[d, half, part] = block
            return 0
        lax.fori_loop(0, SUB, body, 0, unroll=8)

    def stage_in(got, half, part, dest):
        def body(d, _):
            block = got[d, half] if part is None else got[d, half, part]
            dest[pl.ds(pl.multiple_of(d * ROWS + half * GAP, 8), USED), :] = block.astype(F32)
            return 0
        lax.fori_loop(0, SUB, body, 0, unroll=8)

    halves = [range(0, HALF), range(HALF, BAND)]
    first, second = Exchange(0, sent0, got0), Exchange(1, sent1, got1)
    third, fourth = Exchange(2, sent2, got2), Exchange(3, sent3, got3)
    empty = jnp.zeros((64, LONS), BF16)
    loads["fields"].wait()
    loads["dft"].wait()
    for half in range(2):
        for i in halves[half]:
            here = fields[i]
            real = jnp.concatenate([here, empty], axis=0)
            imag = jnp.concatenate([empty, here], axis=0)
            zonal = dot(dft_ref[0:192, :], real, NT) + dot(dft_ref[192:384, :], imag, NT)
            for mm in range(BAND):
                put(spread.at[0], i, mm, zonal[mm * SUB:(mm + 1) * SUB, :])
        stage_out(spread.at[0], sent0, half, None)
        if half == 0:
            pl.semaphore_wait(barrier, SUB + GROUP - 2)
        first.start(half)

    loads["order"].wait()
    loads["place"].wait()
    for mm in range(BAND):
        rows = order_ref[mm]
        col = jnp.concatenate([rows, place_ref[...], jnp.zeros((112, 256), F32)], axis=0).T[0:LATS, :]
        for b in range(4):
            c = col[b * 48:(b + 1) * 48, :]
            top = c[:, 3:4] * rows[1:2, :] - c[:, 4:5] * rows[0:1, :]
            gap = (c[:, 8:9] - place_ref[0:1, :]) + (c[:, 9:10] - place_ref[1:2, :])
            same = c[:, 10:11] == place_ref[2:3, :]
            value = jnp.where(same, rows[2:3, :], top / jnp.where(same, 1.0, gap))
            filt[mm, b * 48:(b + 1) * 48, :] = value.astype(BF16)
    for name in ("enc", "spec", "gain", "up", "down", "proj"):
        loads[name].wait()
    gain[...] = jnp.concatenate([gain_ref[...], jnp.zeros((126, 128), F32)], axis=0).T
    enc = enc_ref[...].T
    none = jnp.zeros((128, 64), BF16)
    enc_real = jnp.concatenate([enc, none], axis=1)
    enc_imag = jnp.concatenate([none, enc], axis=1)
    mix[0] = (dot(spec_ref[0, 0], enc_real, NN) - dot(spec_ref[0, 1], enc_imag, NN)).astype(BF16)
    mix[1] = (dot(spec_ref[0, 1], enc_real, NN) + dot(spec_ref[0, 0], enc_imag, NN)).astype(BF16)

    def latitude(i, part):
        return jnp.concatenate([take(spread.at[part], i, mm) for mm in range(BAND)], axis=0).astype(BF16)

    def apply_filter(parts, sent, exchange):
        for mm in range(BAND):
            for part in range(parts):
                source[mm, :, part * 128:(part + 1) * 128] = jnp.concatenate(
                    [take(spread.at[part], i, mm) for i in range(BAND)], axis=0).astype(BF16)
        for half in range(2):
            for mm in range(BAND):
                filtered = dot(filt[mm, half * 96:(half + 1) * 96, 0:LATS], source[mm, :, 0:parts * 128], NN)
                for part in range(parts):
                    for k, i in enumerate(halves[half]):
                        put(result.at[part], i, mm, filtered[k * SUB:(k + 1) * SUB, part * 128:(part + 1) * 128])
            for part in range(parts):
                stage_out(result.at[part], sent, half, part if parts > 1 else None)
            exchange.start(half)

    for half in range(2):
        first.finish(half)
        stage_in(got0, half, None, spread.at[0])
    apply_filter(1, sent1, second)

    def pointwise(layer, summed):
        centred = summed - jnp.mean(summed, axis=0, keepdims=True)
        spread_of = jnp.mean(centred * centred, axis=0, keepdims=True)
        normed = (centred * lax.rsqrt(spread_of + 1e-05) * gain[:, layer:layer + 1]).astype(BF16)
        lifted = erf_gelu(dot(up_ref[layer], normed, NN)).astype(BF16)
        return (summed + dot(down_ref[layer], lifted, NN)).astype(BF16)

    for half in range(2):
        second.finish(half)
        stage_in(got1, half, None, spread.at[0])
        for i in halves[half]:
            back = latitude(i, 0)
            real = dot(mix[0], back, NT).astype(BF16)
            imag = dot(mix[1], back, NT).astype(BF16)
            summed = dot(enc, fields[i], NN)
            summed = summed + dot(real, dft_ref[0:192, :], NN) + dot(imag, dft_ref[192:384, :], NN)
            after = pointwise(0, summed)
            hidden[i] = after
            zonal = dot(dft_ref[...], after, NT)
            for part in range(2):
                for mm in range(BAND):
                    at = part * 192 + mm * SUB
                    put(result.at[part], i, mm, zonal[at:at + SUB, :])
        for part in range(2):
            stage_out(result.at[part], sent2, half, part)
        third.start(half)

    for half in range(2):
        third.finish(half)
        for part in range(2):
            stage_in(got2, half, part, spread.at[part])
    apply_filter(2, sent3, fourth)

    def second_back(i):
        back_real = latitude(i, 0)
        back_imag = latitude(i, 1)
        w_real, w_imag = spec_ref[1, 0], spec_ref[1, 1]
        real = (dot(w_real, back_real, NT) - dot(w_imag, back_imag, NT)).astype(BF16)
        imag = (dot(w_imag, back_real, NT) + dot(w_real, back_imag, NT)).astype(BF16)
        summed = hidden[i].astype(F32)
        summed = summed + dot(real, dft_ref[0:192, :], NN) + dot(imag, dft_ref[192:384, :], NN)
        ahead = fields[i].astype(F32) + dot(proj_ref[...], pointwise(1, summed), NN)
        for l in range(3):
            cast[3 * i + l] = ahead[:, l * 128:(l + 1) * 128]

    lane = lax.broadcasted_iota(jnp.int32, (8, 128), 1)

    def window(w, begin):
        first, turn = begin // 128, begin % 128
        def piece(j):
            return cast[min(max(j, 0), 17), pl.ds(w, 8, stride=8), :]
        if turn == 0:
            return piece(first)
        return jnp.where(
            lane < 128 - turn, pltpu.roll(piece(first), 128 - turn, 1), pltpu.roll(piece(first + 1), 128 - turn, 1))

    def slice_tile(g):
        columns = []
        for t in range(9):
            value = window(t, 144 * g - 16 * t) if t < 8 else None
            if t > 0:
                before = window(t - 1, 144 * (g + 1) - 16 * t)
                value = before if value is None else jnp.where(lane < 16 * t, before, value)
            columns.append(value)
        tiles[g] = jnp.concatenate(columns, axis=0).astype(BF16)

    def tile_copy(to, origin):
        return pltpu.make_async_remote_copy(
            src_ref=tiles.at[to], dst_ref=out_ref.at[origin], send_sem=tile_send.at[to],
            recv_sem=tile_recv.at[origin], device_id=(to, sub), device_id_type=MESH)

    for half in range(2):
        fourth.finish(half)
        for part in range(2):
            stage_in(got3, half, part, spread.at[part])
        for i in halves[half]:
            second_back(i)
        for g in range(half * 8, half * 8 + 8):
            slice_tile(g)

        def tile_start(d, _):
            to = half * 8 + (group + d) % 8

            @pl.when(to != group)
            def _():
                tile_copy(to, group).start()

            return 0

        lax.fori_loop(0, 8, tile_start, 0)

    def tile_finish(d, _):
        other = (group + d) % GROUP
        tile_copy(other, group).wait_send()
        tile_copy(other, other).wait_recv()
        return 0

    own = pltpu.make_async_copy(tiles.at[group], out_ref.at[group], local_sem.at[10])
    own.start()
    own.wait()
    lax.fori_loop(1, GROUP, tile_finish, 0)


def forecast(ic, enc, spec, gain, up, down, proj):
    order, place = filter_tables()
    hbm = pl.BlockSpec(memory_space=pltpu.HBM)
    block = (SUB, 2, USED, 128)
    pair = (SUB, 2, 2, USED, 128)
    return pl.pallas_call(
        forecast_kernel,
        out_shape=jax.ShapeDtypeStruct((GROUP, 72, 128), BF16),
        in_specs=[hbm] * 10,
        out_specs=pl.BlockSpec(memory_space=pl.ANY),
        scratch_shapes=[
            pltpu.VMEM((BAND, 64, LONS), BF16), pltpu.VMEM((64, 128), BF16), pltpu.VMEM((2, 2, 128, 128), BF16),
            pltpu.VMEM((2, 128), F32), pltpu.VMEM((2, 256, 128), BF16), pltpu.VMEM((2, 128, 256), BF16),
            pltpu.VMEM((64, 128), BF16), pltpu.VMEM((384, LONS), BF16), pltpu.VMEM((8, 256), F32),
            pltpu.VMEM((BAND, 8, 256), F32),
            pltpu.VMEM((BAND, LATS, 256), BF16),
            pltpu.VMEM((128, 128), F32),
            pltpu.VMEM((2, 128, 128), BF16),
            pltpu.VMEM((2, ALL, 128), F32),
            pltpu.VMEM((2, ALL, 128), F32),
            pltpu.VMEM((BAND, LATS, 256), BF16),
            pltpu.VMEM(block, BF16), pltpu.VMEM(block, BF16), pltpu.VMEM(block, BF16), pltpu.VMEM(block, BF16),
            pltpu.VMEM(pair, BF16), pltpu.VMEM(pair, BF16), pltpu.VMEM(pair, BF16), pltpu.VMEM(pair, BF16),
            pltpu.VMEM((BAND, 128, LONS), BF16),
            pltpu.VMEM((18, 64, 128), F32),
            pltpu.VMEM((GROUP, 72, 128), BF16),
            pltpu.SemaphoreType.DMA((8, SUB)), pltpu.SemaphoreType.DMA((8, SUB)),
            pltpu.SemaphoreType.DMA((GROUP,)), pltpu.SemaphoreType.DMA((GROUP,)),
            pltpu.SemaphoreType.DMA((11,)),
        ],
        compiler_params=pltpu.CompilerParams(collective_id=0, has_side_effects=True, vmem_limit_bytes=62 << 20),
        name="forecast",
    )(jnp.transpose(ic, (1, 0, 2)), enc.T, spec, gain, up, down, proj, jnp.asarray(dft_table(), BF16), jnp.asarray(place), jnp.asarray(order))


def reduce_rows(rows, at):
    lines = [rows[a:a + 1, :] for a in range(8)]
    d = [[jnp.broadcast_to(lines[a][:, at + b:at + b + 1], (1, 128)) for b in range(8)] for a in range(8)]
    for p in range(0, 8, 2):
        q = p + 1
        pp, pq, qp, qq = d[p][p], d[p][q], d[q][p], d[q][q]
        scale = 1.0 / (pp * qq - pq * qp)
        pp, pq, qp, qq = qq * scale, pq * scale, qp * scale, pp * scale
        lines[p], lines[q] = pp * lines[p] - pq * lines[q], qq * lines[q] - qp * lines[p]
        later = range(q + 1, 8)
        top = {b: (pp * d[p][b] - pq * d[q][b], qq * d[q][b] - qp * d[p][b]) for b in later}
        for c in range(8):
            if c in (p, q):
                continue
            f, g = d[c][p], d[c][q]
            lines[c] = lines[c] - (f * lines[p] + g * lines[q])
            for b in later:
                d[c][b] = d[c][b] - (f * top[b][0] + g * top[b][1])
        for b in later:
            d[p][b], d[q][b] = top[b]
    return lines


def inverse(block):
    lane = lax.broadcasted_iota(jnp.int32, (64, 128), 1)
    row = lax.broadcasted_iota(jnp.int32, (64, 128), 0)
    both = jnp.where(lane < 64, block, (lane - 64 == row).astype(F32))
    parts = [both[r * 8:(r + 1) * 8, :] for r in range(8)]
    for step in range(8):
        at = step * 8
        lines = reduce_rows(parts[step], at)
        for r in range(8):
            if r == step:
                continue
            x = parts[r]
            c = [jnp.broadcast_to(x[:, at + b:at + b + 1], (8, 128)) for b in range(8)]
            terms = [c[b] * lines[b] for b in range(8)]
            parts[r] = x - (((terms[0] + terms[1]) + (terms[2] + terms[3]))
                            + ((terms[4] + terms[5]) + (terms[6] + terms[7])))
        parts[step] = jnp.concatenate(lines, axis=0)
    return jnp.concatenate(parts, axis=0)[:, 64:128]


def jordan(sys_ref):
    def shifted(left, right, rows):
        lane = lax.broadcasted_iota(jnp.int32, (rows, 128), 1)
        left, right = pltpu.roll(left, 64, 1), pltpu.roll(right, 64, 1)
        return jnp.where(lane < 64, left, right), jnp.where(lane < 64, right, left)

    def step(blk, _):
        at = pl.ds(pl.multiple_of(blk * 64, 64), 64)
        inv = inverse(sys_ref[at, 0:128])
        rows = dot(inv, sys_ref[at, :], NN, EXACT)
        full = sys_ref[...] - dot(sys_ref[:, 0:64], rows, NN, EXACT)
        sys_ref[:, 256:384] = full[:, 256:384]
        sys_ref[:, 0:128], sys_ref[:, 128:256] = shifted(full[:, 0:128], full[:, 128:256], 256)
        sys_ref[at, 256:384] = rows[:, 256:384]
        sys_ref[at, 0:128], sys_ref[at, 128:256] = shifted(rows[:, 0:128], rows[:, 128:256], 64)
        return 0

    lax.fori_loop(0, 4, step, 0)


def analysis_kernel(tile_ref, count_ref, pos_ref, val_ref, var_ref, mod_ref, out_ref, raw, state, pert, sysm, mtab):
    for q in range(16):
        raw[q * 72:(q + 1) * 72, :] = tile_ref[q].astype(F32)
    def collect(r, _):
        rows = raw[pl.ds(r, 16, stride=72), :]
        at = pl.ds(pl.multiple_of(r * 16, 16), 16)
        state[at, :] = rows
        mean = jnp.sum(rows, axis=0, keepdims=True) * (1.0 / 16)
        pert[at, :] = rows - mean
        return 0
    lax.fori_loop(0, 72, collect, 0, unroll=8)
    pos = pos_ref[...]
    col = pos >> 7
    lane = pos & 127
    u = jnp.floor((col.astype(F32) + 0.5) * (1.0 / 9)).astype(jnp.int32)
    row = (col - 9 * u) * 8 + u
    cell = pos - 144 * jnp.floor((pos.astype(F32) + 0.5) * (1.0 / 144)).astype(jnp.int32)
    pick = (lax.broadcasted_iota(jnp.int32, (128, 512), 0) == lane).astype(F32).astype(BF16)
    pick_cell = (lax.broadcasted_iota(jnp.int32, (144, 512), 0) == cell).astype(F32).astype(BF16)
    def gather(i, acc):
        at = pl.ds(pl.multiple_of(i * 128, 128), 128)
        part = dot(state[at, :].astype(BF16), pick, NN)
        for k in range(8):
            acc = acc + jnp.where(row == i * 8 + k, part[k * 16:(k + 1) * 16, :], 0.0)
        return acc
    picked = lax.fori_loop(0, 9, gather, jnp.zeros((16, 512), F32), unroll=True)
    mod = mod_ref[...]
    hi = mod.astype(BF16)
    rest = mod - hi.astype(F32)
    mid = rest.astype(BF16)
    low = (rest - mid.astype(F32)).astype(BF16)
    mod_at = dot(hi, pick_cell, NN) + dot(mid, pick_cell, NN) + dot(low, pick_cell, NN)
    valid = lax.broadcasted_iota(jnp.int32, (1, 512), 1) < count_ref[0, 0]
    root = jnp.where(valid, lax.rsqrt(var_ref[...]), 0.0)
    dev = (picked - jnp.sum(picked, axis=0, keepdims=True) * (1.0 / 16)) * (root * (1.0 / math.sqrt(15.0)))
    innov = jnp.where(valid, val_ref[...] - picked, 0.0) * root
    anom = jnp.concatenate([dev[k:k + 1, :] * mod_at for k in range(16)], axis=0)
    eye = (lax.broadcasted_iota(jnp.int32, (256, 256), 0) == lax.broadcasted_iota(jnp.int32, (256, 256), 1)).astype(F32)
    sysm[:, 0:256] = dot(anom, anom, NT, EXACT) + eye
    rhs = jnp.concatenate([innov, jnp.zeros((112, 512), F32)], axis=0)
    sysm[:, 256:384] = dot(anom, rhs, NT, EXACT)
    jordan(sysm)
    wt = sysm[:, 256:384].T[0:16, :]
    spread = jnp.concatenate([wt] * 16, axis=0)
    same = (lax.broadcasted_iota(jnp.int32, (256, 256), 0) // 16) == (lax.broadcasted_iota(jnp.int32, (256, 256), 1) // 16)
    spread = jnp.where(same, spread, 0.0)
    modk = jnp.concatenate([mod * (1.0 / math.sqrt(15.0))] * 16, axis=0)
    coef = dot(spread, modk, NN, EXACT)
    for t in range(9):
        start = (128 * t) % 144
        if start + 128 <= 144:
            part = coef[:, start:start + 128]
        else:
            part = jnp.concatenate([coef[:, start:144], coef[:, 0:start - 16]], axis=1)
        mtab[t] = part
    def apply(t, _):
        for u8 in range(8):
            at = pl.multiple_of((t * 8 + u8) * 16, 16)
            acc = state[pl.ds(at, 16), :]
            p = pert[pl.ds(at, 16), :]
            for k in range(16):
                acc = acc + mtab[t, k * 16:(k + 1) * 16, :] * p[k:k + 1, :]
            out_ref[:, pl.ds(pl.multiple_of((9 * u8 + t) * 128, 128), 128)] = acc.astype(BF16)
        return 0
    lax.fori_loop(0, 9, apply, 0)


def analysis(tile, count, pos, val, var, mod):
    v = pl.BlockSpec(memory_space=pltpu.VMEM)
    return pl.pallas_call(
        analysis_kernel,
        out_shape=jax.ShapeDtypeStruct((16, 9216), BF16),
        in_specs=[v, pl.BlockSpec(memory_space=pltpu.SMEM), v, v, v, v],
        out_specs=v,
        scratch_shapes=[pltpu.VMEM((1152, 128), F32), pltpu.VMEM((1152, 128), F32), pltpu.VMEM((1152, 128), F32),
                        pltpu.VMEM((256, 384), F32), pltpu.VMEM((9, 256, 128), F32)],
        compiler_params=pltpu.CompilerParams(vmem_limit_bytes=48 << 20),
        name="analysis",
    )(tile, count, pos, val, var, mod)


def shards(ic, enc, spec, gain, up, down, proj, pos, count, value, var, mod):
    tile = forecast(ic[0], enc, spec, gain, up, down, proj)
    out = analysis(tile, count, pos[0], value[0], var[0], mod[0, 0])
    return out[None, None]


def solution(mesh):
    part = P("sub", "group", None)
    return jax.shard_map(
        shards,
        mesh=mesh,
        in_specs=(P("group", None, "sub", None),) + (P(),) * 6
        + (part, P("sub", "group"), part, part, P("sub", "group", None, None)),
        out_specs=P("sub", "group", None, None),
        check_vma=False,
    )
```

```python
import functools
import math

import jax
import jax.numpy as jnp
import numpy as np
from jax import lax
from jax.experimental import pallas as pl
from jax.experimental.pallas import tpu as pltpu
from jax.sharding import PartitionSpec as P

F32 = jnp.float32
BF16 = jnp.bfloat16
EXACT = lax.Precision.HIGHEST
MESH = pl.DeviceIdType.MESH
NN = ((1,), (0,))
NT = ((1,), (1,))

LATS = 192
LONS = 384
DEGREES = 192
SUB = 32
GROUP = 16
BAND = 6
HALF = BAND // 2
USED = HALF * BAND
GAP = 24
ROWS = 2 * GAP
ALL = SUB * ROWS


def dot(a, b, dims, precision=None):
    return lax.dot_general(a, b, (dims, ((), ())), precision=precision, preferred_element_type=F32)


def dft_table():
    m = (BAND * np.arange(SUB)[None, :] + np.arange(BAND)[:, None]).reshape(-1)
    angle = 2.0 * np.pi * ((m[:, None] * np.arange(LONS)[None, :]) % LONS) / LONS
    return np.concatenate([np.cos(angle), -np.sin(angle)], axis=0)


def filter_tables():
    colatitude = (np.arange(LATS) + 0.5) * np.pi / LATS
    x, sine = np.cos(colatitude), np.sin(colatitude)
    m = np.arange(LATS, dtype=np.float64)[:, None]
    gammas = np.array([math.lgamma(v + 0.5) - math.lgamma(v + 1.0) for v in range(LATS)])[:, None]
    start = np.exp(
        0.5 * (np.log((2 * m + 1) / (4 * np.pi)) + gammas - 0.5 * np.log(np.pi)) + m * np.log(sine)[None, :]
    )
    earlier, previous, squares = np.zeros_like(start), np.zeros_like(start), np.zeros_like(start)
    for l in range(DEGREES + 1):
        up = np.sqrt((4.0 * l * l - 1.0) / np.maximum(l * l - m * m, 1.0)) if l else 0.0 * m
        low = np.sqrt(np.maximum((l - 1.0) ** 2 - m * m, 0.0) / max(4.0 * (l - 1.0) ** 2 - 1.0, 1.0))
        value = up * (x[None, :] * previous - low * earlier)
        value = np.where(l == m + 1, x[None, :] * np.sqrt(2 * m + 3) * start, value)
        value = np.where(l == m, start, np.where(l < m, 0.0, value))
        earlier, previous = previous, value
        if l < DEGREES:
            squares += value * value
    weight = 2.0 * np.pi * (np.pi / LATS) * sine[None, :] * np.where(m == 0, 1.0, 2.0) / LONS
    e = np.sqrt((DEGREES**2 - m * m) / (4.0 * DEGREES**2 - 1.0))
    per_order = [previous * e * weight, earlier * e * weight, squares * weight, previous, earlier]
    order = np.zeros((SUB, BAND, 8, 256), np.float32)
    place = np.zeros((8, 256), np.float32)
    place[0] = 2.0 + np.arange(256)
    lats = (BAND * np.arange(SUB)[None, :] + np.arange(BAND)[:, None]).reshape(-1)
    for k, table in enumerate(per_order):
        order[:, :, k, :LATS] = table.reshape(SUB, BAND, LATS)[:, :, lats]
    place[0, :LATS] = x[lats].astype(np.float32)
    place[1, :LATS] = x[lats] - x[lats].astype(np.float32).astype(np.float64)
    place[2] = np.arange(256)
    return order, place


def erf_gelu(x):
    return 0.5 * x * (1.0 + lax.erf(x * (1.0 / math.sqrt(2.0))))


def forecast_kernel(
    ic_hbm, enc_hbm, spec_hbm, gain_hbm, up_hbm, down_hbm, proj_hbm, dft_hbm, place_hbm, order_hbm, out_ref,
    fields, enc_ref, spec_ref, gain_ref, up_ref, down_ref, proj_ref, dft_ref, place_ref, order_ref,
    filt, gain, mix, spread, result, source, sent0, got0, sent1, got1, sent2, got2, sent3, got3,
    hidden, cast, tiles, send_sem, recv_sem, tile_send, tile_recv, local_sem,
):
    group = lax.axis_index("group")
    sub = lax.axis_index("sub")

    barrier = pltpu.get_barrier_semaphore()

    def greet_subs(d, _):
        pl.semaphore_signal(barrier, inc=1, device_id=(group, (sub + d) % SUB), device_id_type=MESH)
        return 0

    def greet_tiles(d, _):
        pl.semaphore_signal(barrier, inc=1, device_id=((group + d) % GROUP, sub), device_id_type=MESH)
        return 0

    lax.fori_loop(1, SUB, greet_subs, 0)
    lax.fori_loop(1, GROUP, greet_tiles, 0)

    loads = {}
    for n, (name, src, dst) in enumerate((
        ("fields", ic_hbm, fields), ("dft", dft_hbm, dft_ref), ("order", order_hbm.at[sub], order_ref),
        ("place", place_hbm, place_ref), ("enc", enc_hbm, enc_ref), ("spec", spec_hbm, spec_ref),
        ("gain", gain_hbm, gain_ref), ("up", up_hbm, up_ref), ("down", down_hbm, down_ref),
        ("proj", proj_hbm, proj_ref),
    )):
        loads[name] = pltpu.make_async_copy(src, dst, local_sem.at[n])
        loads[name].start()

    def far_first(e):
        k = (e // 2) % 8
        z = (sub // 4 + 4 + (k // 2) * (1 - 2 * (k % 2)) - k % 2) % 8
        return z * 4 + (sub // 2 + 1 - e // 16) % 2 * 2 + (sub + 1 + e) % 2

    class Exchange:
        def __init__(self, stage, sent, got):
            self.stage, self.sent, self.got = stage, sent, got

        def copy(self, half, d):
            band = far_first(d)
            return pltpu.make_async_remote_copy(
                src_ref=self.sent.at[band, half], dst_ref=self.got.at[sub, half],
                send_sem=send_sem.at[self.stage * 2 + half, d], recv_sem=recv_sem.at[self.stage * 2 + half, d],
                device_id=(group, band), device_id_type=MESH)

        def start(self, half):
            def body(d, _):
                self.copy(half, d).start()
                return 0

            lax.fori_loop(0, SUB - 1, body, 0)
            self.got[sub, half] = self.sent[sub, half]

        def finish(self, half):
            def body(d, _):
                self.copy(half, d).wait_recv()
                return 0

            lax.fori_loop(0, SUB - 1, body, 0)

        def drain(self):
            def body(d, _):
                self.copy(0, d).wait_send()
                self.copy(1, d).wait_send()
                return 0

            lax.fori_loop(0, SUB - 1, body, 0)

    def row_of(i, mm):
        return (i // HALF) * GAP + (i % HALF) * BAND + mm

    def put(dest, i, mm, rows):
        dest[pl.ds(row_of(i, mm), SUB, stride=ROWS), :] = rows

    def take(src, i, mm):
        return src[pl.ds(row_of(i, mm), SUB, stride=ROWS), :]

    def stage_out(src, sent, half, part):
        def body(d, _):
            block = src[pl.ds(pl.multiple_of(d * ROWS + half * GAP, 8), USED), :].astype(BF16)
            if part is None:
                sent[d, half] = block
            else:
                sent[d, half, part] = block
            return 0
        lax.fori_loop(0, SUB, body, 0, unroll=8)

    def stage_in(got, half, part, dest):
        def body(d, _):
            block = got[d, half] if part is None else got[d, half, part]
            dest[pl.ds(pl.multiple_of(d * ROWS + half * GAP, 8), USED), :] = block.astype(F32)
            return 0
        lax.fori_loop(0, SUB, body, 0, unroll=8)

    halves = [range(0, HALF), range(HALF, BAND)]
    first, second = Exchange(0, sent0, got0), Exchange(1, sent1, got1)
    third, fourth = Exchange(2, sent2, got2), Exchange(3, sent3, got3)
    empty = jnp.zeros((64, LONS), BF16)
    loads["fields"].wait()
    loads["dft"].wait()
    for half in range(2):
        for i in halves[half]:
            here = fields[i]
            real = jnp.concatenate([here, empty], axis=0)
            imag = jnp.concatenate([empty, here], axis=0)
            zonal = dot(dft_ref[0:192, :], real, NT) + dot(dft_ref[192:384, :], imag, NT)
            for mm in range(BAND):
                put(spread.at[0], i, mm, zonal[mm * SUB:(mm + 1) * SUB, :])
        stage_out(spread.at[0], sent0, half, None)
        if half == 0:
            pl.semaphore_wait(barrier, SUB + GROUP - 2)
        first.start(half)

    loads["order"].wait()
    loads["place"].wait()
    for mm in range(BAND):
        rows = order_ref[mm]
        col = jnp.concatenate([rows, place_ref[...], jnp.zeros((112, 256), F32)], axis=0).T[0:LATS, :]
        for b in range(4):
            c = col[b * 48:(b + 1) * 48, :]
            top = c[:, 3:4] * rows[1:2, :] - c[:, 4:5] * rows[0:1, :]
            gap = (c[:, 8:9] - place_ref[0:1, :]) + (c[:, 9:10] - place_ref[1:2, :])
            same = c[:, 10:11] == place_ref[2:3, :]
            value = jnp.where(same, rows[2:3, :], top / jnp.where(same, 1.0, gap))
            filt[mm, b * 48:(b + 1) * 48, :] = value.astype(BF16)
    for name in ("enc", "spec", "gain", "up", "down", "proj"):
        loads[name].wait()
    gain[...] = jnp.concatenate([gain_ref[...], jnp.zeros((126, 128), F32)], axis=0).T
    enc = enc_ref[...].T
    none = jnp.zeros((128, 64), BF16)
    enc_real = jnp.concatenate([enc, none], axis=1)
    enc_imag = jnp.concatenate([none, enc], axis=1)
    mix[0] = (dot(spec_ref[0, 0], enc_real, NN) - dot(spec_ref[0, 1], enc_imag, NN)).astype(BF16)
    mix[1] = (dot(spec_ref[0, 1], enc_real, NN) + dot(spec_ref[0, 0], enc_imag, NN)).astype(BF16)

    def latitude(i, part):
        return jnp.concatenate([take(spread.at[part], i, mm) for mm in range(BAND)], axis=0).astype(BF16)

    def apply_filter(parts, sent, exchange):
        for mm in range(BAND):
            for part in range(parts):
                source[mm, :, part * 128:(part + 1) * 128] = jnp.concatenate(
                    [take(spread.at[part], i, mm) for i in range(BAND)], axis=0).astype(BF16)
        for half in range(2):
            for mm in range(BAND):
                filtered = dot(filt[mm, half * 96:(half + 1) * 96, 0:LATS], source[mm, :, 0:parts * 128], NN)
                for part in range(parts):
                    for k, i in enumerate(halves[half]):
                        put(result.at[part], i, mm, filtered[k * SUB:(k + 1) * SUB, part * 128:(part + 1) * 128])
            for part in range(parts):
                stage_out(result.at[part], sent, half, part if parts > 1 else None)
            exchange.start(half)

    for half in range(2):
        first.finish(half)
        stage_in(got0, half, None, spread.at[0])
    apply_filter(1, sent1, second)

    def pointwise(layer, summed):
        centred = summed - jnp.mean(summed, axis=0, keepdims=True)
        spread_of = jnp.mean(centred * centred, axis=0, keepdims=True)
        normed = (centred * lax.rsqrt(spread_of + 1e-05) * gain[:, layer:layer + 1]).astype(BF16)
        lifted = erf_gelu(dot(up_ref[layer], normed, NN)).astype(BF16)
        return (summed + dot(down_ref[layer], lifted, NN)).astype(BF16)

    for half in range(2):
        second.finish(half)
        stage_in(got1, half, None, spread.at[0])
        for i in halves[half]:
            back = latitude(i, 0)
            real = dot(mix[0], back, NT).astype(BF16)
            imag = dot(mix[1], back, NT).astype(BF16)
            summed = dot(enc, fields[i], NN)
            summed = summed + dot(real, dft_ref[0:192, :], NN) + dot(imag, dft_ref[192:384, :], NN)
            after = pointwise(0, summed)
            hidden[i] = after
            zonal = dot(dft_ref[...], after, NT)
            for part in range(2):
                for mm in range(BAND):
                    at = part * 192 + mm * SUB
                    put(result.at[part], i, mm, zonal[at:at + SUB, :])
        for part in range(2):
            stage_out(result.at[part], sent2, half, part)
        third.start(half)

    for half in range(2):
        third.finish(half)
        for part in range(2):
            stage_in(got2, half, part, spread.at[part])
    apply_filter(2, sent3, fourth)

    def second_back(i):
        back_real = latitude(i, 0)
        back_imag = latitude(i, 1)
        w_real, w_imag = spec_ref[1, 0], spec_ref[1, 1]
        real = (dot(w_real, back_real, NT) - dot(w_imag, back_imag, NT)).astype(BF16)
        imag = (dot(w_imag, back_real, NT) + dot(w_real, back_imag, NT)).astype(BF16)
        summed = hidden[i].astype(F32)
        summed = summed + dot(real, dft_ref[0:192, :], NN) + dot(imag, dft_ref[192:384, :], NN)
        ahead = fields[i].astype(F32) + dot(proj_ref[...], pointwise(1, summed), NN)
        for l in range(3):
            cast[3 * i + l] = ahead[:, l * 128:(l + 1) * 128]

    lane = lax.broadcasted_iota(jnp.int32, (8, 128), 1)

    def window(w, begin):
        first, turn = begin // 128, begin % 128
        def piece(j):
            return cast[min(max(j, 0), 17), pl.ds(w, 8, stride=8), :]
        if turn == 0:
            return piece(first)
        return jnp.where(
            lane < 128 - turn, pltpu.roll(piece(first), 128 - turn, 1), pltpu.roll(piece(first + 1), 128 - turn, 1))

    def slice_tile(g):
        columns = []
        for t in range(9):
            value = window(t, 144 * g - 16 * t) if t < 8 else None
            if t > 0:
                before = window(t - 1, 144 * (g + 1) - 16 * t)
                value = before if value is None else jnp.where(lane < 16 * t, before, value)
            columns.append(value)
        tiles[g] = jnp.concatenate(columns, axis=0).astype(BF16)

    def tile_copy(to, origin):
        return pltpu.make_async_remote_copy(
            src_ref=tiles.at[to], dst_ref=out_ref.at[origin], send_sem=tile_send.at[to],
            recv_sem=tile_recv.at[origin], device_id=(to, sub), device_id_type=MESH)

    for half in range(2):
        fourth.finish(half)
        for part in range(2):
            stage_in(got3, half, part, spread.at[part])
        for i in halves[half]:
            second_back(i)
        for g in range(half * 8, half * 8 + 8):
            slice_tile(g)

        def tile_start(d, _):
            to = half * 8 + (group + d) % 8

            @pl.when(to != group)
            def _():
                tile_copy(to, group).start()

            return 0

        lax.fori_loop(0, 8, tile_start, 0)

    def tile_finish(d, _):
        other = (group + d) % GROUP
        tile_copy(other, group).wait_send()
        tile_copy(other, other).wait_recv()
        return 0

    own = pltpu.make_async_copy(tiles.at[group], out_ref.at[group], local_sem.at[10])
    own.start()
    for done in (first, second, third, fourth):
        done.drain()
    own.wait()
    lax.fori_loop(1, GROUP, tile_finish, 0)


def forecast(ic, enc, spec, gain, up, down, proj):
    order, place = filter_tables()
    hbm = pl.BlockSpec(memory_space=pltpu.HBM)
    block = (SUB, 2, USED, 128)
    pair = (SUB, 2, 2, USED, 128)
    return pl.pallas_call(
        forecast_kernel,
        out_shape=jax.ShapeDtypeStruct((GROUP, 72, 128), BF16),
        in_specs=[hbm] * 10,
        out_specs=pl.BlockSpec(memory_space=pl.ANY),
        scratch_shapes=[
            pltpu.VMEM((BAND, 64, LONS), BF16), pltpu.VMEM((64, 128), BF16), pltpu.VMEM((2, 2, 128, 128), BF16),
            pltpu.VMEM((2, 128), F32), pltpu.VMEM((2, 256, 128), BF16), pltpu.VMEM((2, 128, 256), BF16),
            pltpu.VMEM((64, 128), BF16), pltpu.VMEM((384, LONS), BF16), pltpu.VMEM((8, 256), F32),
            pltpu.VMEM((BAND, 8, 256), F32),
            pltpu.VMEM((BAND, LATS, 256), BF16),
            pltpu.VMEM((128, 128), F32),
            pltpu.VMEM((2, 128, 128), BF16),
            pltpu.VMEM((2, ALL, 128), F32),
            pltpu.VMEM((2, ALL, 128), F32),
            pltpu.VMEM((BAND, LATS, 256), BF16),
            pltpu.VMEM(block, BF16), pltpu.VMEM(block, BF16), pltpu.VMEM(block, BF16), pltpu.VMEM(block, BF16),
            pltpu.VMEM(pair, BF16), pltpu.VMEM(pair, BF16), pltpu.VMEM(pair, BF16), pltpu.VMEM(pair, BF16),
            pltpu.VMEM((BAND, 128, LONS), BF16),
            pltpu.VMEM((18, 64, 128), F32),
            pltpu.VMEM((GROUP, 72, 128), BF16),
            pltpu.SemaphoreType.DMA((8, SUB)), pltpu.SemaphoreType.DMA((8, SUB)),
            pltpu.SemaphoreType.DMA((GROUP,)), pltpu.SemaphoreType.DMA((GROUP,)),
            pltpu.SemaphoreType.DMA((11,)),
        ],
        compiler_params=pltpu.CompilerParams(collective_id=0, has_side_effects=True, vmem_limit_bytes=62 << 20),
        name="forecast",
    )(jnp.transpose(ic, (1, 0, 2)), enc.T, spec, gain, up, down, proj, jnp.asarray(dft_table(), BF16), jnp.asarray(place), jnp.asarray(order))


def reduce_rows(rows, at):
    lines = [rows[a:a + 1, :] for a in range(8)]
    d = [[jnp.broadcast_to(lines[a][:, at + b:at + b + 1], (1, 128)) for b in range(8)] for a in range(8)]
    for p in range(0, 8, 2):
        q = p + 1
        pp, pq, qp, qq = d[p][p], d[p][q], d[q][p], d[q][q]
        scale = 1.0 / (pp * qq - pq * qp)
        pp, pq, qp, qq = qq * scale, pq * scale, qp * scale, pp * scale
        lines[p], lines[q] = pp * lines[p] - pq * lines[q], qq * lines[q] - qp * lines[p]
        later = range(q + 1, 8)
        top = {b: (pp * d[p][b] - pq * d[q][b], qq * d[q][b] - qp * d[p][b]) for b in later}
        for c in range(8):
            if c in (p, q):
                continue
            f, g = d[c][p], d[c][q]
            lines[c] = lines[c] - (f * lines[p] + g * lines[q])
            for b in later:
                d[c][b] = d[c][b] - (f * top[b][0] + g * top[b][1])
        for b in later:
            d[p][b], d[q][b] = top[b]
    return lines


def inverse(block):
    lane = lax.broadcasted_iota(jnp.int32, (64, 128), 1)
    row = lax.broadcasted_iota(jnp.int32, (64, 128), 0)
    both = jnp.where(lane < 64, block, (lane - 64 == row).astype(F32))
    parts = [both[r * 8:(r + 1) * 8, :] for r in range(8)]
    for step in range(8):
        at = step * 8
        lines = reduce_rows(parts[step], at)
        for r in range(8):
            if r == step:
                continue
            x = parts[r]
            c = [jnp.broadcast_to(x[:, at + b:at + b + 1], (8, 128)) for b in range(8)]
            terms = [c[b] * lines[b] for b in range(8)]
            parts[r] = x - (((terms[0] + terms[1]) + (terms[2] + terms[3]))
                            + ((terms[4] + terms[5]) + (terms[6] + terms[7])))
        parts[step] = jnp.concatenate(lines, axis=0)
    return jnp.concatenate(parts, axis=0)[:, 64:128]


def jordan(sys_ref):
    def shifted(left, right, rows):
        lane = lax.broadcasted_iota(jnp.int32, (rows, 128), 1)
        left, right = pltpu.roll(left, 64, 1), pltpu.roll(right, 64, 1)
        return jnp.where(lane < 64, left, right), jnp.where(lane < 64, right, left)

    def step(blk, _):
        at = pl.ds(pl.multiple_of(blk * 64, 64), 64)
        inv = inverse(sys_ref[at, 0:128])
        rows = dot(inv, sys_ref[at, :], NN, EXACT)
        full = sys_ref[...] - dot(sys_ref[:, 0:64], rows, NN, EXACT)
        sys_ref[:, 256:384] = full[:, 256:384]
        sys_ref[:, 0:128], sys_ref[:, 128:256] = shifted(full[:, 0:128], full[:, 128:256], 256)
        sys_ref[at, 256:384] = rows[:, 256:384]
        sys_ref[at, 0:128], sys_ref[at, 128:256] = shifted(rows[:, 0:128], rows[:, 128:256], 64)
        return 0

    lax.fori_loop(0, 4, step, 0)


def analysis_kernel(tile_ref, count_ref, pos_ref, val_ref, var_ref, mod_ref, out_ref, raw, state, pert, sysm, mtab):
    for q in range(16):
        raw[q * 72:(q + 1) * 72, :] = tile_ref[q].astype(F32)
    def collect(r, _):
        rows = raw[pl.ds(r, 16, stride=72), :]
        at = pl.ds(pl.multiple_of(r * 16, 16), 16)
        state[at, :] = rows
        mean = jnp.sum(rows, axis=0, keepdims=True) * (1.0 / 16)
        pert[at, :] = rows - mean
        return 0
    lax.fori_loop(0, 72, collect, 0, unroll=8)
    pos = pos_ref[...]
    col = pos >> 7
    lane = pos & 127
    u = jnp.floor((col.astype(F32) + 0.5) * (1.0 / 9)).astype(jnp.int32)
    row = (col - 9 * u) * 8 + u
    cell = pos - 144 * jnp.floor((pos.astype(F32) + 0.5) * (1.0 / 144)).astype(jnp.int32)
    pick = (lax.broadcasted_iota(jnp.int32, (128, 512), 0) == lane).astype(F32).astype(BF16)
    pick_cell = (lax.broadcasted_iota(jnp.int32, (144, 512), 0) == cell).astype(F32).astype(BF16)
    def gather(i, acc):
        at = pl.ds(pl.multiple_of(i * 128, 128), 128)
        part = dot(state[at, :].astype(BF16), pick, NN)
        for k in range(8):
            acc = acc + jnp.where(row == i * 8 + k, part[k * 16:(k + 1) * 16, :], 0.0)
        return acc
    picked = lax.fori_loop(0, 9, gather, jnp.zeros((16, 512), F32), unroll=True)
    mod = mod_ref[...]
    hi = mod.astype(BF16)
    rest = mod - hi.astype(F32)
    mid = rest.astype(BF16)
    low = (rest - mid.astype(F32)).astype(BF16)
    mod_at = dot(hi, pick_cell, NN) + dot(mid, pick_cell, NN) + dot(low, pick_cell, NN)
    valid = lax.broadcasted_iota(jnp.int32, (1, 512), 1) < count_ref[0, 0]
    root = jnp.where(valid, lax.rsqrt(var_ref[...]), 0.0)
    dev = (picked - jnp.sum(picked, axis=0, keepdims=True) * (1.0 / 16)) * (root * (1.0 / math.sqrt(15.0)))
    innov = jnp.where(valid, val_ref[...] - picked, 0.0) * root
    anom = jnp.concatenate([dev[k:k + 1, :] * mod_at for k in range(16)], axis=0)
    eye = (lax.broadcasted_iota(jnp.int32, (256, 256), 0) == lax.broadcasted_iota(jnp.int32, (256, 256), 1)).astype(F32)
    sysm[:, 0:256] = dot(anom, anom, NT, EXACT) + eye
    rhs = jnp.concatenate([innov, jnp.zeros((112, 512), F32)], axis=0)
    sysm[:, 256:384] = dot(anom, rhs, NT, EXACT)
    jordan(sysm)
    wt = sysm[:, 256:384].T[0:16, :]
    spread = jnp.concatenate([wt] * 16, axis=0)
    same = (lax.broadcasted_iota(jnp.int32, (256, 256), 0) // 16) == (lax.broadcasted_iota(jnp.int32, (256, 256), 1) // 16)
    spread = jnp.where(same, spread, 0.0)
    modk = jnp.concatenate([mod * (1.0 / math.sqrt(15.0))] * 16, axis=0)
    coef = dot(spread, modk, NN, EXACT)
    for t in range(9):
        start = (128 * t) % 144
        if start + 128 <= 144:
            part = coef[:, start:start + 128]
        else:
            part = jnp.concatenate([coef[:, start:144], coef[:, 0:start - 16]], axis=1)
        mtab[t] = part
    def apply(t, _):
        for u8 in range(8):
            at = pl.multiple_of((t * 8 + u8) * 16, 16)
            acc = state[pl.ds(at, 16), :]
            p = pert[pl.ds(at, 16), :]
            for k in range(16):
                acc = acc + mtab[t, k * 16:(k + 1) * 16, :] * p[k:k + 1, :]
            out_ref[:, pl.ds(pl.multiple_of((9 * u8 + t) * 128, 128), 128)] = acc.astype(BF16)
        return 0
    lax.fori_loop(0, 9, apply, 0)


def analysis(tile, count, pos, val, var, mod):
    v = pl.BlockSpec(memory_space=pltpu.VMEM)
    return pl.pallas_call(
        analysis_kernel,
        out_shape=jax.ShapeDtypeStruct((16, 9216), BF16),
        in_specs=[v, pl.BlockSpec(memory_space=pltpu.SMEM), v, v, v, v],
        out_specs=v,
        scratch_shapes=[pltpu.VMEM((1152, 128), F32), pltpu.VMEM((1152, 128), F32), pltpu.VMEM((1152, 128), F32),
                        pltpu.VMEM((256, 384), F32), pltpu.VMEM((9, 256, 128), F32)],
        compiler_params=pltpu.CompilerParams(vmem_limit_bytes=48 << 20),
        name="analysis",
    )(tile, count, pos, val, var, mod)


def shards(ic, enc, spec, gain, up, down, proj, pos, count, value, var, mod):
    tile = forecast(ic[0], enc, spec, gain, up, down, proj)
    out = analysis(tile, count, pos[0], value[0], var[0], mod[0, 0])
    return out[None, None]


def solution(mesh):
    part = P("sub", "group", None)
    return jax.shard_map(
        shards,
        mesh=mesh,
        in_specs=(P("group", None, "sub", None),) + (P(),) * 6
        + (part, P("sub", "group"), part, part, P("sub", "group", None, None)),
        out_specs=P("sub", "group", None, None),
        check_vma=False,
    )
```
